32 devices in a mesh: grp: 8 (over z, y), ep: 4 (over x, core).
Axes of the slice: x: 2, y: 2, z: 4, core: 2. Of those that a mesh axis runs over, the one named last changes fastest.
Arguments:
- tokens: bfloat16 [6144, 4096], P(('grp', 'ep')), may hold values from -6 to 6
- expert_ids: int32 [6144, 8], P(('grp', 'ep')), may hold values from 0 to 127, all different within a row; in each aligned block of 192 rows (0 to 191, 192 to 383, ...) at most 24 rows name the same one
- gate_probs: float32 [6144, 8], P(('grp', 'ep')), may hold values from 0.02 to 0.25
- placement: int32 [8, 1], P('grp'), may hold values from 0 to 1
- gate_weight: bfloat16 [8, 4096, 768], P('grp', None, 'ep'), may hold values from -0.09375 to 0.09375
- up_weight: bfloat16 [8, 4096, 768], P('grp', None, 'ep'), may hold values from -0.09375 to 0.09375
- down_weight: bfloat16 [8, 768, 4096], P('grp', 'ep'), may hold values from -0.21875 to 0.21875
- out_grad: bfloat16 [6144, 4096], P(('grp', 'ep')), may hold values from -6 to 6
- moment_first: float32 [2, 768, 4096], P(None, 'ep', 'grp'), may hold values from -2 to 2
- moment_second: float32 [2, 768, 4096], P(None, 'ep', 'grp'), may hold values from 0.01 to 1
Outputs:
- token_grad: bfloat16 [6144, 4096], P(('grp', 'ep'))
- step_dir: bfloat16 [8, 768, 4096], P('grp', 'ep')
- new_first: float32 [2, 768, 4096], P(None, 'ep', 'grp')
- new_second: float32 [2, 768, 4096], P(None, 'ep', 'grp')
The draws below stay inside these ranges and needn't reach their ends.
Inputs may be any that keep to these rules, and one draw needn't show every extreme that they name: `expert_ids`: each row names 8 different experts. In the rows of one device no expert is named more than 24 times, a bound that some block reaches. Group g holds expert placement[g, s] + s in its slot s.
All inputs are finite; a program needn't handle non-finite values.
Results may differ from the reference program's by a relative error of at most 0.015.
Values may be sent and summed in bfloat16 or wider, within the bound.
No kernel may reach another device: no remote copies, remote signals or barrier semaphores. Data moves between devices by JAX's collectives and lax.ppermute only.
A program may use at most 128 MiB of HBM per device.

```python
import math
import jax
import jax.numpy as jnp
import numpy as np
from jax import lax

D = 4096
HID = 768
EXPERTS = 128
TOP = 8
QUARTERS = 4
CANDS = 2
TOK_DEV = 192
SLOTS = 1
H_DEV = 192
CAP = 24
TOKENS = 6144
N_GRP = 8
N_EP = 4


def with_ends(result, own_key, least, top_value):
    dims = result.shape
    place = [jax.random.randint(jax.random.fold_in(own_key, axis), (), 0, dims[axis]) for axis in range(len(dims))]
    result = result.at[tuple(place)].set(least)
    longest = dims.index(max(dims))
    place[longest] = (place[longest] + 1) % dims[longest]
    return result.at[tuple(place)].set(top_value)


def levels(key, dims, shards, low, largest):
    def one(axis_at, blocks):
        draws = jax.random.uniform(jax.random.fold_in(jax.random.fold_in(key, 6), axis_at), (blocks,), jnp.float32, low / len(shards), largest / len(shards))
        return jnp.repeat(jnp.exp(draws), dims[axis_at] // blocks).reshape((-1,) + (1,) * (len(dims) - axis_at - 1))

    loudness = one(*shards[0])
    for cut in shards[1:]:
        loudness = loudness * one(*cut)
    return loudness


def shared_out(key, own, number, rows, amount, top, reach, slope):
    order = jax.random.permutation(key, amount)
    packed, usual = portions_of(amount, rows * top, reach, slope, True), portions_of(amount, rows * top, reach, slope, False)
    places = jnp.arange(amount)

    def named(tallies, turn):
        used = int((tallies > 0).sum())
        fixed = max(1, used // 4)
        moved = fixed + (places - fixed + turn * (used - fixed)) % max(1, amount - fixed)
        return jnp.zeros((amount,), jnp.int32).at[order[jnp.where(places < fixed, places, moved)]].set(jnp.asarray(tallies, jnp.int32))

    tallies = jnp.where(number % 4 == 0, named(packed, number // 4), named(usual, number - number // 4 - 1))
    mixed = jax.random.permutation(jax.random.fold_in(own, 3), amount)
    source_of, receiver = mixed[0:amount // 2 * 2:2], mixed[1:amount // 2 * 2:2]
    slack = jnp.minimum(tallies[source_of] - 1, reach - tallies[receiver]) // 2
    slack = jnp.where((source_of == order[0]) | (receiver == order[0]) | (tallies[receiver] == 0), 0, jnp.maximum(slack, 0))
    moved = jax.random.randint(jax.random.fold_in(own, 4), (amount // 2,), 0, 1 << 20) % (slack + 1)
    tallies = tallies.at[source_of].add(-moved).at[receiver].add(moved)
    members = jnp.searchsorted(jnp.cumsum(tallies), jnp.arange(rows * top), side="right").astype(jnp.int32)
    table = members.reshape(top, rows).T
    table = table[jax.random.permutation(jax.random.fold_in(own, 1), rows)]
    turn = jax.random.randint(jax.random.fold_in(own, 2), (rows, 1), 0, top)
    return jnp.take_along_axis(table, (jnp.arange(top)[None, :] + turn) % top, axis=1)


def portions_of(count, total, limit, skew, full):
    weights = [(1 << 20) // math.isqrt(grade ** skew) + 1 for grade in range(1, count + 1)]
    largest = limit if full else min(limit, max(-(-total // count), total * weights[0] // sum(weights)))
    least = 1 if total - largest >= count - 1 else 0
    counts, surplus = [largest] + [least] * (count - 1), total - largest - least * (count - 1)
    while surplus > 0:
        movable = [i for i in range(1, count) if counts[i] < largest] or [i for i in range(1, count) if counts[i] < limit]
        mass, budget = sum([weights[i] for i in movable]), surplus
        for i in movable:
            extra = min(limit - counts[i], max(1, budget * weights[i] // mass), surplus)
            counts[i] = counts[i] + extra
            surplus = surplus - extra
    return np.array(counts)


def scatter_about(key, dims, deviation, bound, split=(), held_as=jnp.bfloat16):
    entries = deviation * jax.random.normal(key, dims, jnp.float32)
    if split:
        entries = entries * levels(key, dims, split, -0.22, 0.18)
    return jnp.clip(entries, -bound, bound).astype(held_as)


def setup_inputs(seed: int = 0) -> dict:
    arg_keys = jax.random.split(jax.random.key(seed), 11)
    tokens = scatter_about(arg_keys[0], (TOKENS, D), 1.0, 6.0, ((0, 32),))
    expert_ids_keys = jax.random.split(jax.random.fold_in(arg_keys[1], 1), TOKENS // TOK_DEV)
    expert_ids_turns = jax.random.permutation(jax.random.fold_in(arg_keys[1], 3), TOKENS // TOK_DEV)
    expert_ids = jax.vmap(lambda own, number: shared_out(jax.random.fold_in(arg_keys[1], 2), own, number, TOK_DEV, EXPERTS, TOP, CAP, 2))(expert_ids_keys, expert_ids_turns).reshape((TOKENS, TOP))
    gate_probs = jnp.clip(0.02 + 0.23 * jax.random.uniform(arg_keys[2], (TOKENS, TOP), jnp.float32) ** levels(arg_keys[2], (TOKENS, TOP), ((0, 32),), -0.2, 0.2), 0.02, 0.25)
    placement = with_ends(jax.random.randint(arg_keys[3], (N_GRP, SLOTS), 0, CANDS), jax.random.fold_in(arg_keys[3], 1), 0, CANDS - 1).astype(jnp.int32)
    gate_weight = scatter_about(arg_keys[4], (N_GRP, D, N_EP * H_DEV), D ** -0.5, 0.09375, ((0, 8), (2, 4)))
    up_weight = scatter_about(arg_keys[5], (N_GRP, D, N_EP * H_DEV), D ** -0.5, 0.09375, ((0, 8), (2, 4)))
    down_weight = scatter_about(arg_keys[6], (N_GRP, N_EP * H_DEV, D), HID ** -0.5, 0.21875, ((0, 8), (1, 4)))
    out_grad = scatter_about(arg_keys[7], (TOKENS, D), 1.0, 6.0, ((0, 32),))
    moment_first = scatter_about(arg_keys[8], (CANDS, N_EP * H_DEV, D), 0.3, 2.0, ((1, 4), (2, 8)), jnp.float32)
    moment_second = jnp.clip(jnp.exp(math.log(1.0) - 4.6051702 * jax.random.uniform(arg_keys[9], (CANDS, N_EP * H_DEV, D), jnp.float32) ** levels(arg_keys[9], (CANDS, N_EP * H_DEV, D), ((1, 4), (2, 8)), -0.2, 0.2)), 0.01, 1.0)
    return dict(tokens=tokens, expert_ids=expert_ids, gate_probs=gate_probs, placement=placement, gate_weight=gate_weight, up_weight=up_weight, down_weight=down_weight, out_grad=out_grad, moment_first=moment_first, moment_second=moment_second)


beta_one = 0.9
beta_two = 0.999
adam_eps = 1e-08
first_fix = 1.0 - math.exp(1000.0 * math.log(0.9))
second_fix = 1.0 - math.exp(1000.0 * math.log(0.999))

def adam_step(gradient, first_moment, second):
    new_first = beta_one * first_moment + (1.0 - beta_one) * gradient
    new_second = beta_two * second + (1.0 - beta_two) * gradient * gradient
    direction = new_first / first_fix / (jnp.sqrt(new_second / second_fix) + adam_eps)
    return (new_first, new_second, direction)

def one_group(inputs):
    tok_rows, id_rows, prob_rows, grad_rows, place_row, gate_group, up_group, down_group = inputs
    count_rows = tok_rows.shape[0]
    token_acc = jnp.zeros((count_rows, D), jnp.float32)
    grad_list = []
    for slot_index in range(SLOTS):
        expert = place_row[slot_index] * SLOTS + slot_index
        matches = id_rows == expert
        coeffs = lax.optimization_barrier(jnp.sum(jnp.where(matches, prob_rows, jnp.float32(0.0)), axis=1))
        hit_rows = jnp.any(matches, axis=1)
        chosen = jnp.nonzero(hit_rows, size=N_EP * CAP, fill_value=0)[0].astype(jnp.int32)
        valid = jnp.arange(N_EP * CAP, dtype=jnp.int32) < jnp.sum(hit_rows.astype(jnp.int32))
        sel_coeffs = jnp.where(valid, coeffs[chosen], jnp.float32(0.0))
        sel_tokens = tok_rows[chosen]
        sel_grads = grad_rows[chosen]
        w_gate = gate_group[:, slot_index * HID:(slot_index + 1) * HID]
        w_up = up_group[:, slot_index * HID:(slot_index + 1) * HID]
        w_down = down_group[slot_index * HID:(slot_index + 1) * HID, :]
        pre_gate = jnp.dot(sel_tokens, w_gate, preferred_element_type=jnp.float32)
        pre_up = jnp.dot(sel_tokens, w_up, preferred_element_type=jnp.float32)
        sigmoid_gate = jax.nn.sigmoid(pre_gate)
        activated = pre_gate * sigmoid_gate
        hidden = (activated * pre_up).astype(jnp.bfloat16)
        scaled = (sel_coeffs[:, None] * sel_grads.astype(jnp.float32)).astype(jnp.bfloat16)
        d_hidden = jnp.dot(scaled, w_down.T, preferred_element_type=jnp.float32)
        grad_list.append(jnp.dot(hidden.T, scaled, preferred_element_type=jnp.float32))
        d_gate = (d_hidden * pre_up * sigmoid_gate * (1.0 + pre_gate * (1.0 - sigmoid_gate))).astype(jnp.bfloat16)
        d_up = (d_hidden * activated).astype(jnp.bfloat16)
        quarter_sum = jnp.zeros((N_EP * CAP, D), jnp.float32)
        for quarter in range(QUARTERS):
            low = quarter * H_DEV
            high = low + H_DEV
            partial_value = jnp.dot(d_gate[:, low:high], w_gate[:, low:high].T, preferred_element_type=jnp.float32)
            partial_value = partial_value + jnp.dot(d_up[:, low:high], w_up[:, low:high].T, preferred_element_type=jnp.float32)
            rounded = lax.optimization_barrier(partial_value.astype(jnp.bfloat16))
            quarter_sum = quarter_sum + rounded.astype(jnp.float32)
        token_acc = token_acc.at[chosen].add(quarter_sum)
    return (token_acc.astype(jnp.bfloat16), jnp.stack(grad_list))

def reference(tokens, expert_ids, gate_probs, placement, gate_weight, up_weight, down_weight, out_grad, moment_first, moment_second):
    group_rows = N_EP * TOK_DEV
    per_group = (tokens.reshape(N_GRP, group_rows, D), expert_ids.reshape(N_GRP, group_rows, TOP), gate_probs.reshape(N_GRP, group_rows, TOP), out_grad.reshape(N_GRP, group_rows, D), placement, gate_weight, up_weight, down_weight)
    token_grad, slot_grads = lax.map(one_group, per_group)
    chosen_cands = (placement[:, :, None] == jnp.arange(CANDS, dtype=jnp.int32)[None, None, :]).astype(jnp.float32)
    summed = jnp.einsum('gsr,gshd->rshd', chosen_cands, slot_grads, precision=lax.Precision.HIGHEST)
    summed = summed.reshape(CANDS, SLOTS * HID, D)
    new_first, new_second, direction = adam_step(summed, moment_first, moment_second)
    copy_dirs = jnp.einsum('gsr,rshd->gshd', chosen_cands, direction.reshape(CANDS, SLOTS, HID, D), precision=lax.Precision.HIGHEST)
    step_dir = copy_dirs.reshape(N_GRP, SLOTS * HID, D).astype(jnp.bfloat16)
    return (token_grad.reshape(N_GRP * group_rows, D), step_dir, new_first, new_second)
```

```python
import functools
import math

import jax
import jax.numpy as jnp
from jax import lax
from jax.experimental import pallas as pl
from jax.experimental.pallas import tpu as pltpu
from jax.sharding import PartitionSpec as P

QUARTERS = 4
CANDS = 2
CAP = 24
TAG = 16


beta_one = 0.9
beta_two = 0.999
adam_eps = 1e-08
first_fix = 1.0 - math.exp(1000.0 * math.log(0.9))
second_fix = 1.0 - math.exp(1000.0 * math.log(0.999))

F32 = jnp.float32
BF16 = jnp.bfloat16
NT = (((1,), (1,)), ((), ()))
TN = (((0,), (0,)), ((), ()))


def cost(flops, moved):
    return pl.CostEstimate(flops=int(flops), bytes_accessed=int(moved), transcendentals=0)


def rows_of(parts):
    return jnp.concatenate([part.astype(F32) for part in parts], axis=0).astype(BF16)


def select_kernel(slots, place, ids, probs, tokens, rows, mask, coefs):
    tok = ids.shape[1]

    @pl.when(pl.program_id(0) == 0)
    def _():
        below = lax.broadcasted_iota(jnp.int32, (tok, tok), 0)
        right = lax.broadcasted_iota(jnp.int32, (tok, tok), 1)
        upper = jnp.where(below <= right, 1.0, 0.0).astype(BF16)
        for slot in range(slots):
            held = place[0, slot] * slots + slot
            match = ids[...] == held
            hit = jnp.max(jnp.where(match, 1.0, 0.0), axis=0, keepdims=True)
            coef = jnp.sum(jnp.where(match, probs[...], 0.0), axis=0, keepdims=True)
            rank = jnp.dot(hit.astype(BF16), upper, preferred_element_type=F32)
            want = lax.broadcasted_iota(jnp.int32, (CAP, tok), 0).astype(F32) + 1.0
            chosen = jnp.where((rank == want) & (hit > 0.0), 1.0, 0.0)
            at = slice(slot * CAP, (slot + 1) * CAP)
            mask[at, :] = chosen.astype(BF16)
            total = jnp.sum(chosen * coef, axis=1, keepdims=True)
            coefs[at, :] = jnp.broadcast_to(total, (CAP, coefs.shape[1]))

    rows[...] = jnp.dot(mask[...], tokens[...], preferred_element_type=F32).astype(BF16)


def select(placement, ids, probs, tokens, slots):
    tok, width = tokens.shape
    step = width // 4
    count = slots * CAP
    return pl.pallas_call(
        functools.partial(select_kernel, slots),
        grid=(width // step,),
        in_specs=[
            pl.BlockSpec(memory_space=pltpu.SMEM),
            pl.BlockSpec(ids.shape, lambda i: (0, 0)),
            pl.BlockSpec(probs.shape, lambda i: (0, 0)),
            pl.BlockSpec((tok, step), lambda i: (0, i)),
        ],
        out_specs=[
            pl.BlockSpec((count, step), lambda i: (0, i)),
            pl.BlockSpec((count, tok), lambda i: (0, 0)),
            pl.BlockSpec((count, 128), lambda i: (0, 0)),
        ],
        out_shape=[
            jax.ShapeDtypeStruct((count, width), BF16),
            jax.ShapeDtypeStruct((count, tok), BF16),
            jax.ShapeDtypeStruct((count, 128), F32),
        ],
        cost_estimate=cost(2 * count * tok * width, tok * width * 2),
        name="select_rows",
    )(placement, ids, probs, tokens)


def scale_kernel(mask, coefs, grads, rows, blocks):
    picked = jnp.dot(mask[...], grads[...], preferred_element_type=F32)
    scaled = (coefs[:, 0:1] * picked).astype(BF16)
    rows[...] = scaled
    blocks[0] = scaled


def scale(mask, coefs, grads, groups):
    tok, width = grads.shape
    step = width // groups
    count = mask.shape[0]
    return pl.pallas_call(
        scale_kernel,
        grid=(groups,),
        in_specs=[
            pl.BlockSpec(mask.shape, lambda i: (0, 0)),
            pl.BlockSpec(coefs.shape, lambda i: (0, 0)),
            pl.BlockSpec((tok, step), lambda i: (0, i)),
        ],
        out_specs=[
            pl.BlockSpec((count, step), lambda i: (0, i)),
            pl.BlockSpec((1, count, step), lambda i: (i, 0, 0)),
        ],
        out_shape=[
            jax.ShapeDtypeStruct((count, width), BF16),
            jax.ShapeDtypeStruct((groups, count, step), BF16),
        ],
        cost_estimate=cost(2 * count * tok * width, tok * width * 2),
        name="scale_rows",
    )(mask, coefs, grads)


def forward_kernel(parts, place, *refs):
    blocks, (w_gate, w_up, pre_gate, pre_up, hidden) = refs[:parts], refs[parts:]
    step = pl.program_id(0)

    @pl.when(step == 0)
    def _():
        pre_gate[...] = jnp.zeros_like(pre_gate)
        pre_up[...] = jnp.zeros_like(pre_up)

    inputs = rows_of([block[...] for block in blocks])
    pre_gate[...] += lax.dot_general(inputs, w_gate[...], NT, preferred_element_type=F32)
    pre_up[...] += lax.dot_general(inputs, w_up[...], NT, preferred_element_type=F32)

    @pl.when(step == pl.num_programs(0) - 1)
    def _():
        gate = pre_gate[...]
        count = gate.shape[0]
        hidden[0:count, :] = (gate * jax.nn.sigmoid(gate) * pre_up[...]).astype(BF16)
        tag = place[0, 0].astype(F32)
        hidden[count : count + TAG, :] = jnp.full((TAG, gate.shape[1]), tag, F32).astype(BF16)


def forward(my_cand, blocks, w_gate, w_up):
    units, width = w_gate.shape
    count = len(blocks) * CAP
    step = width // 4
    whole = lambda i: (0, 0)
    return pl.pallas_call(
        functools.partial(forward_kernel, len(blocks)),
        grid=(width // step,),
        in_specs=[pl.BlockSpec(memory_space=pltpu.SMEM)]
        + [pl.BlockSpec((CAP, step), lambda i: (0, i)) for _ in blocks]
        + [pl.BlockSpec((units, step), lambda i: (0, i))] * 2,
        out_specs=[
            pl.BlockSpec((count, units), whole),
            pl.BlockSpec((count, units), whole),
            pl.BlockSpec((count + TAG, units), whole),
        ],
        out_shape=[
            jax.ShapeDtypeStruct((count, units), F32),
            jax.ShapeDtypeStruct((count, units), F32),
            jax.ShapeDtypeStruct((count + TAG, units), BF16),
        ],
        cost_estimate=cost(4 * count * units * width, 4 * units * width),
        name="forward",
    )(my_cand, *blocks, w_gate, w_up)


def adam_kernel(groups, parts, me, *refs):
    hiddens, refs = refs[:groups], refs[groups:]
    blocks, refs = refs[:parts], refs[parts:]
    first, second, new_first, new_second = refs[:4]
    dirs = refs[4:]
    count = parts * CAP
    rights = []
    lefts = [[] for _ in range(CANDS)]
    for peer in range(groups):
        held = hiddens[peer]
        body = held[0:count, :].astype(F32)
        tag = held[count : count + TAG, :].astype(F32)[0:1, :]
        for cand in range(CANDS):
            lefts[cand].append(jnp.where(tag == float(cand), body, 0.0))
        for part in range(parts):
            rights.append(blocks[part][me[0, 0] ^ peer].astype(F32))
    right = jnp.concatenate(rights, axis=0).astype(BF16)
    dir_list = []
    for cand in range(CANDS):
        left = jnp.concatenate(lefts[cand], axis=0).astype(BF16)
        grad = lax.dot_general(left, right, TN, preferred_element_type=F32)
        one = beta_one * first[cand] + (1.0 - beta_one) * grad
        two = beta_two * second[cand] + (1.0 - beta_two) * grad * grad
        new_first[cand] = one
        new_second[cand] = two
        dir_list.append((one / first_fix / (jnp.sqrt(two / second_fix) + adam_eps)).astype(BF16))
    for peer in range(groups):
        tag = hiddens[peer][count : count + TAG, :].astype(F32)[0:1, 0:1]
        out = dir_list[0].astype(F32)
        for cand in range(1, CANDS):
            out = jnp.where(tag == float(cand), dir_list[cand].astype(F32), out)
        dirs[peer][...] = out.astype(BF16)


def adam(me, hiddens, blocks, first, second):
    groups, parts = len(hiddens), len(blocks)
    units, columns = first.shape[1:]
    step = 128
    moment = pl.BlockSpec((CANDS, units, step), lambda i: (0, 0, i))
    rows = groups * parts * CAP
    return pl.pallas_call(
        functools.partial(adam_kernel, groups, parts),
        grid=(columns // step,),
        in_specs=[pl.BlockSpec(memory_space=pltpu.SMEM)]
        + [pl.BlockSpec(one.shape, lambda i: (0, 0)) for one in hiddens]
        + [pl.BlockSpec((groups, CAP, step), lambda i: (0, 0, i)) for _ in blocks]
        + [moment, moment],
        out_specs=[moment, moment] + [pl.BlockSpec((units, step), lambda i: (0, i))] * groups,
        out_shape=[jax.ShapeDtypeStruct(first.shape, F32)] * 2
        + [jax.ShapeDtypeStruct((units, columns), BF16)] * groups,
        cost_estimate=cost(2 * CANDS * rows * units * columns, 16 * first.size),
        name="adam",
    )(me, *hiddens, *blocks, first, second)


def backward_kernel(parts, steps, *refs):
    blocks, refs = refs[:parts], refs[parts:]
    w_down, w_gate, w_up, pre_gate, pre_up = refs[:5]
    outs, (acc, d_gate, d_up) = refs[5 : 5 + parts], refs[5 + parts :]
    step = pl.program_id(0)

    @pl.when(step == 0)
    def _():
        acc[...] = jnp.zeros_like(acc)

    @pl.when(step < steps)
    def _():
        inputs = rows_of([block[...] for block in blocks])
        acc[...] += lax.dot_general(inputs, w_down[...], NT, preferred_element_type=F32)

    @pl.when(step == steps - 1)
    def _():
        gate, up, d_hidden = pre_gate[...], pre_up[...], acc[...]
        sig = jax.nn.sigmoid(gate)
        d_gate[...] = (d_hidden * up * sig * (1.0 + gate * (1.0 - sig))).astype(BF16)
        d_up[...] = (d_hidden * (gate * sig)).astype(BF16)

    @pl.when(step >= steps)
    def _():
        out = jnp.dot(d_gate[...], w_gate[...], preferred_element_type=F32)
        out = out + jnp.dot(d_up[...], w_up[...], preferred_element_type=F32)
        for part in range(parts):
            outs[part][...] = out[part * CAP : (part + 1) * CAP, :].astype(BF16)


def backward(blocks, w_down, w_gate, w_up, pre_gate, pre_up):
    units, width = w_down.shape
    parts = len(blocks)
    count = parts * CAP
    steps = 4
    step = width // steps
    early = lambda i: (0, jnp.minimum(i, steps - 1))
    late = lambda i: (0, jnp.maximum(i - steps, 0))
    whole = lambda i: (0, 0)
    return pl.pallas_call(
        functools.partial(backward_kernel, parts, steps),
        grid=(2 * steps,),
        in_specs=[pl.BlockSpec((CAP, step), early) for _ in blocks]
        + [pl.BlockSpec((units, step), early)]
        + [pl.BlockSpec((units, step), late)] * 2
        + [pl.BlockSpec((count, units), whole)] * 2,
        out_specs=[pl.BlockSpec((CAP, step), late)] * parts,
        out_shape=[jax.ShapeDtypeStruct((CAP, width), BF16)] * parts,
        scratch_shapes=[
            pltpu.VMEM((count, units), F32),
            pltpu.VMEM((count, units), BF16),
            pltpu.VMEM((count, units), BF16),
        ],
        cost_estimate=cost(6 * count * units * width, 6 * units * width),
        name="backward",
    )(*blocks, w_down, w_gate, w_up, pre_gate, pre_up)


def combine_kernel(parts, mask, *refs):
    blocks, out = refs[:parts], refs[parts]
    rows = rows_of([block[...] for block in blocks])
    out[...] = lax.dot_general(mask[...], rows, TN, preferred_element_type=F32).astype(BF16)


def combine(mask, blocks):
    count, tok = mask.shape
    width = blocks[0].shape[1]
    step = width // 4
    return pl.pallas_call(
        functools.partial(combine_kernel, len(blocks)),
        grid=(width // step,),
        in_specs=[pl.BlockSpec((count, tok), lambda i: (0, 0))]
        + [pl.BlockSpec((CAP, step), lambda i: (0, i)) for _ in blocks],
        out_specs=pl.BlockSpec((tok, step), lambda i: (0, i)),
        out_shape=jax.ShapeDtypeStruct((tok, width), BF16),
        cost_estimate=cost(2 * count * tok * width, 2 * tok * width),
        name="combine",
    )(mask, *blocks)


def place_kernel(groups, me, *refs):
    blocks, out, sems = refs[:groups], refs[groups], refs[groups + 1]
    columns = blocks[0].shape[1]
    copies = []
    for peer in range(groups):
        start = pl.multiple_of((me[0, 0] ^ peer) * columns, 128)
        copies.append(
            pltpu.make_async_copy(
                blocks[peer], out.at[:, pl.ds(start, columns)], sems.at[peer]
            )
        )
        copies[-1].start()
    for copy in copies:
        copy.wait()


def place_blocks(me, blocks):
    groups = len(blocks)
    units, columns = blocks[0].shape
    return pl.pallas_call(
        functools.partial(place_kernel, groups),
        in_specs=[pl.BlockSpec(memory_space=pltpu.SMEM)]
        + [pl.BlockSpec(memory_space=pltpu.VMEM)] * groups,
        out_specs=pl.BlockSpec(memory_space=pl.ANY),
        out_shape=jax.ShapeDtypeStruct((units, groups * columns), BF16),
        scratch_shapes=[pltpu.SemaphoreType.DMA((groups,))],
        cost_estimate=cost(0, 4 * groups * units * columns),
        name="place_blocks",
    )(me, *blocks)


def swap(value, axis, size, bits):
    return lax.ppermute(value, axis, [(i, i ^ bits) for i in range(size)])


def body(
    tokens,
    expert_ids,
    gate_probs,
    placement,
    gate_weight,
    up_weight,
    down_weight,
    out_grad,
    moment_first,
    moment_second,
):
    num_ep = lax.axis_size("ep")
    groups = lax.axis_size("grp")
    slots = num_ep // QUARTERS
    ep_index = lax.axis_index("ep")
    me = lax.axis_index("grp").astype(jnp.int32).reshape(1, 1)
    tok = tokens.shape[0]

    def slot_of(bits):
        return (ep_index ^ bits) // QUARTERS

    def of_slot(value, bits, axis):
        if slots == 1:
            return lax.squeeze(value, (axis,))
        return lax.dynamic_index_in_dim(value, slot_of(bits), axis, keepdims=False)

    def share(value, axis):
        got = [None] * num_ep
        for far in range(0, num_ep, 2):
            piece = of_slot(value, far, axis)
            got[far] = swap(piece, "ep", num_ep, far) if far else piece
        for far in range(0, num_ep, 2):
            got[far + 1] = swap(got[far], "ep", num_ep, 1)
        return got

    def per_slot(value):
        return value.reshape((slots, CAP) + value.shape[1:])

    w_gate = gate_weight[0].T
    w_up = up_weight[0].T
    w_down = down_weight[0]

    rows, mask, coefs = select(placement, expert_ids.T, gate_probs.T, tokens, slots)
    in_rows = share(per_slot(rows), 0)
    scaled, scaled_blocks = scale(mask, coefs, out_grad, groups)
    columns = lax.all_to_all(scaled_blocks, "grp", split_axis=0, concat_axis=0, tiled=True)
    columns = share(columns.reshape(groups, slots, CAP, columns.shape[-1]), 1)
    my_cand = lax.dynamic_index_in_dim(placement, slot_of(0), 1, keepdims=True)
    if slots == 1:
        my_cand = placement
    pre_gate, pre_up, hidden = forward(my_cand, in_rows, w_gate, w_up)
    hiddens = [hidden] + [swap(hidden, "grp", groups, bits) for bits in range(1, groups)]
    new_first, new_second, *dirs = adam(me, hiddens, columns, moment_first, moment_second)
    dirs = [dirs[0]] + [swap(dirs[bits], "grp", groups, bits) for bits in range(1, groups)]

    in_scaled = share(per_slot(scaled), 0)
    partials = backward(in_scaled, w_down, w_gate, w_up, pre_gate, pre_up)
    returned = [partials[0]] + [swap(partials[b], "ep", num_ep, b) for b in range(1, num_ep)]
    masks = per_slot(mask)
    spread = jnp.concatenate([of_slot(masks, bits, 0) for bits in range(num_ep)], axis=0)
    token_grad = combine(spread, returned)
    step_dir = place_blocks(me, dirs)[None]
    return (token_grad, step_dir, new_first, new_second)


def solution(mesh):
    return jax.shard_map(
        body,
        mesh=mesh,
        in_specs=(
            P(("grp", "ep"), None),
            P(("grp", "ep"), None),
            P(("grp", "ep"), None),
            P("grp", None),
            P("grp", None, "ep"),
            P("grp", None, "ep"),
            P("grp", "ep", None),
            P(("grp", "ep"), None),
            P(None, "ep", "grp"),
            P(None, "ep", "grp"),
        ),
        out_specs=(
            P(("grp", "ep"), None),
            P("grp", "ep", None),
            P(None, "ep", "grp"),
            P(None, "ep", "grp"),
        ),
        check_vma=False,
    )
```

```python
import functools
import math

import jax
import jax.numpy as jnp
from jax import lax
from jax.experimental import pallas as pl
from jax.experimental.pallas import tpu as pltpu
from jax.sharding import PartitionSpec as P


QUARTERS = 4
CANDS = 2
CAP = 24
TAG = 16


beta_one = 0.9
beta_two = 0.999
adam_eps = 1e-08
first_fix = 1.0 - math.exp(1000.0 * math.log(0.9))
second_fix = 1.0 - math.exp(1000.0 * math.log(0.999))

F32 = jnp.float32
BF16 = jnp.bfloat16
NT = (((1,), (1,)), ((), ()))
TN = (((0,), (0,)), ((), ()))


SCALARS = pl.BlockSpec(memory_space=pltpu.SMEM)
LOCAL = pl.BlockSpec(memory_space=pltpu.VMEM)
PARAMS = pltpu.CompilerParams(vmem_limit_bytes=16 * 2**20)


def cost(flops, moved):
    return pl.CostEstimate(flops=int(flops), bytes_accessed=int(moved), transcendentals=0)


def rows_of(parts):
    return jnp.concatenate([part.astype(F32) for part in parts], axis=0).astype(BF16)


def select_kernel(slots, pieces, place, ids, probs, tokens, rows, mask, coefs, held, sems):
    tok, width = tokens.shape
    step = width // pieces
    copies = []
    for piece in range(pieces):
        at = slice(piece * step, (piece + 1) * step)
        copy = pltpu.make_async_copy(tokens.at[:, at], held.at[:, at], sems.at[piece])
        copy.start()
        copies.append(copy)
    below = lax.broadcasted_iota(jnp.int32, (tok, tok), 0)
    right = lax.broadcasted_iota(jnp.int32, (tok, tok), 1)
    upper = jnp.where(below <= right, 1.0, 0.0).astype(BF16)
    for slot in range(slots):
        expert = place[0, slot] * slots + slot
        match = ids[...] == expert
        hit = jnp.max(jnp.where(match, 1.0, 0.0), axis=0, keepdims=True)
        coef = jnp.sum(jnp.where(match, probs[...], 0.0), axis=0, keepdims=True)
        rank = jnp.dot(hit.astype(BF16), upper, preferred_element_type=F32)
        want = lax.broadcasted_iota(jnp.int32, (CAP, tok), 0).astype(F32) + 1.0
        chosen = jnp.where((rank == want) & (hit > 0.0), 1.0, 0.0)
        at = slice(slot * CAP, (slot + 1) * CAP)
        mask[at, :] = chosen.astype(BF16)
        total = jnp.sum(chosen * coef, axis=1, keepdims=True)
        coefs[at, :] = jnp.broadcast_to(total, (CAP, coefs.shape[1]))
    left = mask[...]
    for piece in range(pieces):
        at = slice(piece * step, (piece + 1) * step)
        copies[piece].wait()
        rows[:, at] = jnp.dot(left, held[:, at], preferred_element_type=F32).astype(BF16)


def select(placement, ids, probs, tokens, slots):
    tok, width = tokens.shape
    pieces = 4
    count = slots * CAP
    return pl.pallas_call(
        functools.partial(select_kernel, slots, pieces),
        in_specs=[SCALARS, LOCAL, LOCAL, pl.BlockSpec(memory_space=pltpu.HBM)],
        out_specs=[LOCAL] * 3,
        out_shape=[
            jax.ShapeDtypeStruct((count, width), BF16),
            jax.ShapeDtypeStruct((count, tok), BF16),
            jax.ShapeDtypeStruct((count, 128), F32),
        ],
        scratch_shapes=[pltpu.VMEM((tok, width), BF16), pltpu.SemaphoreType.DMA((pieces,))],
        compiler_params=PARAMS,
        cost_estimate=cost(2 * count * tok * width, tok * width * 2),
        name="select_rows",
    )(placement, ids, probs, tokens)


def scale_kernel(mask, coefs, grads, rows, blocks):
    groups, _, step = blocks.shape
    left = mask[...]
    coef = coefs[:, 0:1]
    for block in range(groups):
        at = slice(block * step, (block + 1) * step)
        picked = jnp.dot(left, grads[:, at], preferred_element_type=F32)
        scaled = (coef * picked).astype(BF16)
        rows[:, at] = scaled
        blocks[block] = scaled


def scale(mask, coefs, grads, groups):
    tok, width = grads.shape
    count = mask.shape[0]
    return pl.pallas_call(
        scale_kernel,
        in_specs=[LOCAL] * 3,
        out_specs=[LOCAL] * 2,
        out_shape=[
            jax.ShapeDtypeStruct((count, width), BF16),
            jax.ShapeDtypeStruct((groups, count, width // groups), BF16),
        ],
        compiler_params=PARAMS,
        cost_estimate=cost(2 * count * tok * width, tok * width * 2),
        name="scale_rows",
    )(mask, coefs, grads)


def forward_kernel(parts, place, *refs):
    blocks, (w_gate, w_up, pre_gate, pre_up, hidden) = refs[:parts], refs[parts:]
    inputs = rows_of([block[...] for block in blocks])
    gate = lax.dot_general(inputs, w_gate[...], NT, preferred_element_type=F32)
    up = lax.dot_general(inputs, w_up[...], NT, preferred_element_type=F32)
    pre_gate[...] = gate
    pre_up[...] = up
    count = gate.shape[0]
    hidden[0:count, :] = (gate * jax.nn.sigmoid(gate) * up).astype(BF16)
    tag = place[0, 0].astype(F32)
    hidden[count : count + TAG, :] = jnp.full((TAG, gate.shape[1]), tag, F32).astype(BF16)


def forward(my_cand, blocks, w_gate, w_up):
    units, width = w_gate.shape
    count = len(blocks) * CAP
    return pl.pallas_call(
        functools.partial(forward_kernel, len(blocks)),
        in_specs=[SCALARS] + [LOCAL] * (len(blocks) + 2),
        out_specs=[LOCAL] * 3,
        out_shape=[
            jax.ShapeDtypeStruct((count, units), F32),
            jax.ShapeDtypeStruct((count, units), F32),
            jax.ShapeDtypeStruct((count + TAG, units), BF16),
        ],
        compiler_params=PARAMS,
        cost_estimate=cost(4 * count * units * width, 4 * units * width),
        name="forward",
    )(my_cand, *blocks, w_gate, w_up)


def adam_kernel(groups, parts, me, *refs):
    hiddens, refs = refs[:groups], refs[groups:]
    blocks, refs = refs[:parts], refs[parts:]
    first, second, summed = refs[:3]
    dirs = refs[3:]
    count = parts * CAP
    rights = []
    lefts = [[] for _ in range(CANDS)]
    for peer in range(groups):
        held = hiddens[peer]
        part_rows = held[0:count, :].astype(F32)
        tag = held[count : count + TAG, :].astype(F32)[0:1, :]
        for cand in range(CANDS):
            lefts[cand].append(jnp.where(tag == float(cand), part_rows, 0.0))
        for part in range(parts):
            rights.append(blocks[part][me[0, 0] ^ peer].astype(F32))
    right = jnp.concatenate(rights, axis=0).astype(BF16)
    dir_list = []
    for cand in range(CANDS):
        left = jnp.concatenate(lefts[cand], axis=0).astype(BF16)
        grad = lax.dot_general(left, right, TN, preferred_element_type=F32)
        summed[cand] = grad
        one, two = moments(grad, first[cand], second[cand])
        dir_list.append(one / first_fix / (jnp.sqrt(two / second_fix) + adam_eps))
    for peer in range(groups):
        tag = hiddens[peer][count : count + TAG, :].astype(F32)[0:1, 0:1]
        out = dir_list[0]
        for cand in range(1, CANDS):
            out = jnp.where(tag == float(cand), dir_list[cand], out)
        dirs[peer][...] = out.astype(BF16)


def moments(gradient, first_moment, second):
    new_first = beta_one * first_moment + (1.0 - beta_one) * gradient
    new_second = beta_two * second + (1.0 - beta_two) * gradient * gradient
    return (new_first, new_second)


def adam(me, hiddens, blocks, first, second):
    groups, parts = len(hiddens), len(blocks)
    units, columns = first.shape[1:]
    rows = groups * parts * CAP
    return pl.pallas_call(
        functools.partial(adam_kernel, groups, parts),
        in_specs=[SCALARS] + [LOCAL] * (groups + parts + 2),
        out_specs=[LOCAL] * (1 + groups),
        out_shape=[jax.ShapeDtypeStruct(first.shape, F32)]
        + [jax.ShapeDtypeStruct((units, columns), BF16)] * groups,
        compiler_params=PARAMS,
        cost_estimate=cost(2 * CANDS * rows * units * columns, 8 * first.size),
        name="adam",
    )(me, *hiddens, *blocks, first, second)


def backward_kernel(parts, *refs):
    blocks, refs = refs[:parts], refs[parts:]
    w_down, w_gate, w_up, pre_gate, pre_up = refs[:5]
    outs = refs[5:]
    inputs = rows_of([block[...] for block in blocks])
    d_hidden = lax.dot_general(inputs, w_down[...], NT, preferred_element_type=F32)
    gate, up = pre_gate[...], pre_up[...]
    sig = jax.nn.sigmoid(gate)
    d_gate = (d_hidden * up * sig * (1.0 + gate * (1.0 - sig))).astype(BF16)
    d_up = (d_hidden * (gate * sig)).astype(BF16)
    width = w_gate.shape[1]
    step = width // 4
    for piece in range(4):
        at = slice(piece * step, (piece + 1) * step)
        out = jnp.dot(d_gate, w_gate[:, at], preferred_element_type=F32)
        out = out + jnp.dot(d_up, w_up[:, at], preferred_element_type=F32)
        for part in range(parts):
            outs[part][:, at] = out[part * CAP : (part + 1) * CAP, :].astype(BF16)


def backward(blocks, w_down, w_gate, w_up, pre_gate, pre_up):
    units, width = w_down.shape
    parts = len(blocks)
    count = parts * CAP
    return pl.pallas_call(
        functools.partial(backward_kernel, parts),
        in_specs=[LOCAL] * (parts + 5),
        out_specs=[LOCAL] * parts,
        out_shape=[jax.ShapeDtypeStruct((CAP, width), BF16)] * parts,
        compiler_params=PARAMS,
        cost_estimate=cost(6 * count * units * width, 6 * units * width),
        name="backward",
    )(*blocks, w_down, w_gate, w_up, pre_gate, pre_up)


def combine_kernel(parts, pieces, *refs):
    masks, blocks, out, held, sems = refs[0], refs[1 : 1 + parts], *refs[1 + parts :]
    width = out.shape[1]
    step = width // pieces
    left = masks[...]
    copies = []
    for piece in range(pieces):
        at = slice(piece * step, (piece + 1) * step)
        rows = rows_of([block[:, at] for block in blocks])
        held[:, at] = lax.dot_general(left, rows, TN, preferred_element_type=F32).astype(BF16)
        copy = pltpu.make_async_copy(held.at[:, at], out.at[:, at], sems.at[piece])
        copy.start()
        copies.append(copy)
    for copy in copies:
        copy.wait()


def combine(masks, blocks):
    count, tok = masks.shape
    width = blocks[0].shape[1]
    pieces = 4
    return pl.pallas_call(
        functools.partial(combine_kernel, len(blocks), pieces),
        in_specs=[LOCAL] * (1 + len(blocks)),
        out_specs=pl.BlockSpec(memory_space=pltpu.HBM),
        out_shape=jax.ShapeDtypeStruct((tok, width), BF16),
        scratch_shapes=[pltpu.VMEM((tok, width), BF16), pltpu.SemaphoreType.DMA((pieces,))],
        compiler_params=PARAMS,
        cost_estimate=cost(2 * count * tok * width, 2 * tok * width),
        name="combine",
    )(masks, *blocks)


def place_kernel(groups, me, *refs):
    blocks, out, sems = refs[:groups], refs[groups], refs[groups + 1]
    columns = blocks[0].shape[1]
    copies = []
    for peer in range(groups):
        start = pl.multiple_of((me[0, 0] ^ peer) * columns, 128)
        copies.append(
            pltpu.make_async_copy(
                blocks[peer], out.at[:, pl.ds(start, columns)], sems.at[peer]
            )
        )
        copies[-1].start()
    for copy in copies:
        copy.wait()


def place_blocks(me, blocks):
    groups = len(blocks)
    units, columns = blocks[0].shape
    return pl.pallas_call(
        functools.partial(place_kernel, groups),
        in_specs=[SCALARS] + [LOCAL] * groups,
        out_specs=pl.BlockSpec(memory_space=pltpu.HBM),
        out_shape=jax.ShapeDtypeStruct((units, groups * columns), BF16),
        scratch_shapes=[pltpu.SemaphoreType.DMA((groups,))],
        compiler_params=PARAMS,
        cost_estimate=cost(0, 4 * groups * units * columns),
        name="place_blocks",
    )(me, *blocks)


def swap(value, axis, size, bits):
    return lax.ppermute(value, axis, [(i, i ^ bits) for i in range(size)])


def body(
    tokens,
    expert_ids,
    gate_probs,
    placement,
    gate_weight,
    up_weight,
    down_weight,
    out_grad,
    moment_first,
    moment_second,
):
    num_ep = lax.axis_size("ep")
    groups = lax.axis_size("grp")
    slots = num_ep // QUARTERS
    ep_index = lax.axis_index("ep")
    me = lax.axis_index("grp").astype(jnp.int32).reshape(1, 1)

    def slot_of(bits):
        return (ep_index ^ bits) // QUARTERS

    def of_slot(value, bits, axis):
        if slots == 1:
            return lax.squeeze(value, (axis,))
        return lax.dynamic_index_in_dim(value, slot_of(bits), axis, keepdims=False)

    def share(value, axis):
        got = [None] * num_ep
        for far in range(0, num_ep, 2):
            piece = of_slot(value, far, axis)
            got[far] = swap(piece, "ep", num_ep, far) if far else piece
        for far in range(0, num_ep, 2):
            got[far + 1] = swap(got[far], "ep", num_ep, 1)
        return got

    def exchange(values):
        got = [values[0]]
        for bits in range(1, groups):
            got.append(swap(values[bits], "grp", groups, bits))
        return got

    def per_slot(value):
        return value.reshape((slots, CAP) + value.shape[1:])

    w_gate = gate_weight[0].T
    w_up = up_weight[0].T
    w_down = down_weight[0]

    rows, mask, coefs = select(placement, expert_ids.T, gate_probs.T, tokens, slots)
    in_rows = share(per_slot(rows), 0)
    scaled, blocks = scale(mask, coefs, out_grad, groups)
    columns = lax.all_to_all(blocks, "grp", split_axis=0, concat_axis=0, tiled=True)
    columns = share(columns.reshape(groups, slots, CAP, columns.shape[-1]), 1)
    my_cand = placement
    if slots > 1:
        my_cand = lax.dynamic_index_in_dim(placement, slot_of(0), 1, keepdims=True)
    pre_gate, pre_up, hidden = forward(my_cand, in_rows, w_gate, w_up)
    hiddens = exchange([hidden] * groups)
    summed, *dirs = adam(me, hiddens, columns, moment_first, moment_second)
    got_dirs = exchange(dirs)
    new_first, new_second = moments(summed, moment_first, moment_second)

    in_scaled = share(per_slot(scaled), 0)
    partials = backward(in_scaled, w_down, w_gate, w_up, pre_gate, pre_up)
    returned = [partials[0]]
    for bits in range(1, num_ep):
        returned.append(swap(partials[bits], "ep", num_ep, bits))
    masks = per_slot(mask)
    masks = jnp.concatenate([of_slot(masks, bits, 0) for bits in range(num_ep)], axis=0)
    token_grad = combine(masks, returned)
    step_dir = place_blocks(me, got_dirs)[None]
    return (token_grad, step_dir, new_first, new_second)


def solution(mesh):
    return jax.shard_map(
        body,
        mesh=mesh,
        in_specs=(
            P(("grp", "ep"), None),
            P(("grp", "ep"), None),
            P(("grp", "ep"), None),
            P("grp", None),
            P("grp", None, "ep"),
            P("grp", None, "ep"),
            P("grp", "ep", None),
            P(("grp", "ep"), None),
            P(None, "ep", "grp"),
            P(None, "ep", "grp"),
        ),
        out_specs=(
            P(("grp", "ep"), None),
            P("grp", "ep", None),
            P(None, "ep", "grp"),
            P(None, "ep", "grp"),
        ),
        check_vma=False,
    )
```

```python
import functools
import math

import jax
import jax.numpy as jnp
from jax import lax
from jax.experimental import pallas as pl
from jax.experimental.pallas import tpu as pltpu
from jax.sharding import PartitionSpec as P


QUARTERS = 4
CANDS = 2
CAP = 24
TAG = 16


beta_one = 0.9
beta_two = 0.999
adam_eps = 1e-08
first_fix = 1.0 - math.exp(1000.0 * math.log(0.9))
second_fix = 1.0 - math.exp(1000.0 * math.log(0.999))

F32 = jnp.float32
BF16 = jnp.bfloat16
NT = (((1,), (1,)), ((), ()))
TN = (((0,), (0,)), ((), ()))


SCALARS = pl.BlockSpec(memory_space=pltpu.SMEM)
LOCAL = pl.BlockSpec(memory_space=pltpu.VMEM)
FAR = pl.BlockSpec(memory_space=pltpu.HBM)
PARAMS = pltpu.CompilerParams(vmem_limit_bytes=12 * 2**20)
GRANT1 = pltpu.CompilerParams(vmem_limit_bytes=65_400_000)
GRANT2 = pltpu.CompilerParams(vmem_limit_bytes=56_000_000)


def cost(flops, moved):
    return pl.CostEstimate(flops=int(flops), bytes_accessed=int(moved) * 16, transcendentals=0)


def rows_of(parts):
    return jnp.concatenate([part.astype(F32) for part in parts], axis=0).astype(BF16)


def select_kernel(slots, pieces, place, ids, probs, tokens, rows, picks, *refs):
    ids_in, probs_in, tokens_in, sems = refs
    tok, width = tokens.shape
    step = width // pieces
    at = [slice(piece * step, (piece + 1) * step) for piece in range(pieces)]
    pairs = [(ids, ids_in), (probs, probs_in)]
    pairs += [(tokens.at[:, at[i]], tokens_in.at[:, at[i]]) for i in range(pieces)]
    copies = []
    for number, (source, target) in enumerate(pairs):
        copies.append(pltpu.make_async_copy(source, target, sems.at[number]))
        copies[-1].start()
    below = lax.broadcasted_iota(jnp.int32, (tok, tok), 0)
    right = lax.broadcasted_iota(jnp.int32, (tok, tok), 1)
    upper = jnp.where(below <= right, 1.0, 0.0).astype(BF16)
    want = lax.broadcasted_iota(jnp.int32, (CAP, tok), 0).astype(F32) + 1.0
    for copy in copies[:2]:
        copy.wait()
    chosen_list = []
    for slot in range(slots):
        expert = place[0, slot] * slots + slot
        match = ids_in[...] == expert
        hit = jnp.max(jnp.where(match, 1.0, 0.0), axis=0, keepdims=True)
        coef = jnp.sum(jnp.where(match, probs_in[...], 0.0), axis=0, keepdims=True)
        rank = jnp.dot(hit.astype(BF16), upper, preferred_element_type=F32)
        chosen = jnp.where((rank == want) & (hit > 0.0), 1.0, 0.0)
        chosen_list.append(chosen)
        picks[slot * CAP : (slot + 1) * CAP, :] = chosen * coef
    left = jnp.concatenate(chosen_list, axis=0) if slots > 1 else chosen_list[0]
    left = left.astype(BF16)
    for i in range(pieces):
        copies[2 + i].wait()
        picked = jnp.dot(left, tokens_in[:, at[i]], preferred_element_type=F32)
        rows[:, at[i]] = picked.astype(BF16)


def select(placement, ids, probs, tokens, slots):
    tok, width = tokens.shape
    pieces = 4
    count = slots * CAP
    return pl.pallas_call(
        functools.partial(select_kernel, slots, pieces),
        in_specs=[SCALARS] + [FAR] * 3,
        out_specs=[LOCAL] * 2,
        out_shape=[
            jax.ShapeDtypeStruct((count, width), BF16),
            jax.ShapeDtypeStruct((count, tok), F32),
        ],
        scratch_shapes=[
            pltpu.VMEM(ids.shape, ids.dtype),
            pltpu.VMEM(probs.shape, probs.dtype),
            pltpu.VMEM((tok, width), BF16),
            pltpu.SemaphoreType.DMA((2 + pieces,)),
        ],
        compiler_params=GRANT1,
        cost_estimate=cost(2 * count * tok * width, tok * width * 2),
        name="select_rows",
    )(placement, ids, probs, tokens)


def scale_kernel(pieces, picks, grads, scaled, *refs):
    me = lax.axis_index("grp")
    blocks, (grads_in, sems) = refs[:-2], refs[-2:]
    groups = 2 * len(blocks)
    width = grads.shape[1]
    block, step = width // groups, width // pieces
    at = [slice(piece * step, (piece + 1) * step) for piece in range(pieces)]
    copies = []
    for i in range(pieces):
        copies.append(
            pltpu.make_async_copy(grads.at[:, at[i]], grads_in.at[:, at[i]], sems.at[i])
        )
        copies[-1].start()
    coefs = jnp.sum(picks[...], axis=1, keepdims=True)
    left = jnp.where(picks[...] > 0.0, 1.0, 0.0).astype(BF16)
    for i in range(pieces):
        copies[i].wait()
        picked = jnp.dot(left, grads_in[:, at[i]], preferred_element_type=F32)
        scaled[:, at[i]] = (coefs * picked).astype(BF16)
    for group in range(groups):
        start = pl.multiple_of((me ^ group) * block, 128)
        blocks[group // 2][group % 2] = scaled[:, pl.ds(start, block)]


def scale(picks, grads, groups):
    tok, width = grads.shape
    pieces = 4
    count = picks.shape[0]
    pairs = groups // 2
    return pl.pallas_call(
        functools.partial(scale_kernel, pieces),
        in_specs=[LOCAL, FAR],
        out_specs=[LOCAL] * (1 + pairs),
        out_shape=[jax.ShapeDtypeStruct((count, width), BF16)]
        + [jax.ShapeDtypeStruct((2, count, width // groups), BF16)] * pairs,
        scratch_shapes=[pltpu.VMEM((tok, width), BF16), pltpu.SemaphoreType.DMA((pieces,))],
        compiler_params=GRANT2,
        cost_estimate=cost(2 * count * tok * width, tok * width * 8),
        name="scale_rows",
    )(picks, grads)


def stack_kernel(count, *refs):
    for number in range(count):
        for pick, out in enumerate(refs[count:]):
            out[number] = refs[number][pick]


def stack(pairs):
    shape = (len(pairs),) + pairs[0].shape[1:]
    return pl.pallas_call(
        functools.partial(stack_kernel, len(pairs)),
        in_specs=[LOCAL] * len(pairs),
        out_specs=[LOCAL] * 2,
        out_shape=[jax.ShapeDtypeStruct(shape, BF16)] * 2,
        compiler_params=PARAMS,
        cost_estimate=cost(0, 2 * len(pairs) * pairs[0].size),
        name="stack",
    )(*pairs)


def join_kernel(one, two, out):
    count = one.shape[0]
    out[0:count] = one[...]
    out[count:] = two[...]


def join(one, two):
    shape = (one.shape[0] + two.shape[0],) + one.shape[1:]
    return pl.pallas_call(
        join_kernel,
        in_specs=[LOCAL] * 2,
        out_specs=LOCAL,
        out_shape=jax.ShapeDtypeStruct(shape, BF16),
        compiler_params=PARAMS,
        cost_estimate=cost(0, 8 * one.size),
        name="join",
    )(one, two)


def forward_kernel(parts, place, *refs):
    blocks, (w_gate, w_up, pre_gate, pre_up, hidden) = refs[:parts], refs[parts:]
    inputs = rows_of([block[...] for block in blocks])
    gate = lax.dot_general(inputs, w_gate[...], NT, preferred_element_type=F32)
    up = lax.dot_general(inputs, w_up[...], NT, preferred_element_type=F32)
    pre_gate[...] = gate
    pre_up[...] = up
    count = gate.shape[0]
    hidden[0:count, :] = (gate * jax.nn.sigmoid(gate) * up).astype(BF16)
    tag = place[0, 0].astype(F32)
    hidden[count : count + TAG, :] = jnp.full((TAG, gate.shape[1]), tag, F32).astype(BF16)


def forward(my_cand, blocks, w_gate, w_up):
    units, width = w_gate.shape
    count = len(blocks) * CAP
    return pl.pallas_call(
        functools.partial(forward_kernel, len(blocks)),
        in_specs=[SCALARS] + [LOCAL] * (len(blocks) + 2),
        out_specs=[LOCAL] * 3,
        out_shape=[
            jax.ShapeDtypeStruct((count, units), F32),
            jax.ShapeDtypeStruct((count, units), F32),
            jax.ShapeDtypeStruct((count + TAG, units), BF16),
        ],
        compiler_params=PARAMS,
        cost_estimate=cost(4 * count * units * width, 4 * units * width),
        name="forward",
    )(my_cand, *blocks, w_gate, w_up)


def adam_kernel(groups, parts, *refs):
    half = groups // 2
    hiddens, refs = refs[:groups], refs[groups:]
    near, other, first, second, summed = refs[:5]
    dirs = refs[5:]
    count = parts * CAP
    rights = []
    lefts = [[] for _ in range(CANDS)]
    for peer in range(groups):
        held = hiddens[peer]
        part_rows = held[0:count, :].astype(F32)
        tag = held[count : count + TAG, :].astype(F32)[0:1, :]
        for cand in range(CANDS):
            lefts[cand].append(jnp.where(tag == float(cand), part_rows, 0.0))
        for part in range(parts):
            stack = (near, other)[part % 2]
            at = part // 2 * groups + peer // 2 + peer % 2 * half
            rights.append(stack[at].astype(F32))
    right = jnp.concatenate(rights, axis=0).astype(BF16)
    dir_list = []
    for cand in range(CANDS):
        left = jnp.concatenate(lefts[cand], axis=0).astype(BF16)
        grad = lax.dot_general(left, right, TN, preferred_element_type=F32)
        summed[cand] = grad
        one, two = moments(grad, first[cand], second[cand])
        dir_list.append(one / first_fix / (jnp.sqrt(two / second_fix) + adam_eps))
    for peer in range(groups):
        tag = hiddens[peer][count : count + TAG, :].astype(F32)[0:1, 0:1]
        out = dir_list[0]
        for cand in range(1, CANDS):
            out = jnp.where(tag == float(cand), dir_list[cand], out)
        dirs[peer][...] = out.astype(BF16)


def moments(gradient, first_moment, second):
    new_first = beta_one * first_moment + (1.0 - beta_one) * gradient
    new_second = beta_two * second + (1.0 - beta_two) * gradient * gradient
    return (new_first, new_second)


def adam(hiddens, blocks, first, second):
    groups = len(hiddens)
    parts = 2 * blocks[0].shape[0] // groups
    units, columns = first.shape[1:]
    rows = groups * parts * CAP
    return pl.pallas_call(
        functools.partial(adam_kernel, groups, parts),
        in_specs=[LOCAL] * (groups + 4),
        out_specs=[LOCAL] * (1 + groups),
        out_shape=[jax.ShapeDtypeStruct(first.shape, F32)]
        + [jax.ShapeDtypeStruct((units, columns), BF16)] * groups,
        compiler_params=PARAMS,
        cost_estimate=cost(2 * CANDS * rows * units * columns, 8 * first.size),
        name="adam",
    )(*hiddens, *blocks, first, second)


def update_kernel(summed, first, second, new_first, new_second, one_out, two_out, sems):
    copies = []
    for cand in range(CANDS):
        one_out[cand], two_out[cand] = moments(summed[cand], first[cand], second[cand])
        for number, (source, target) in enumerate([(one_out, new_first), (two_out, new_second)]):
            copy = pltpu.make_async_copy(
                source.at[cand], target.at[cand], sems.at[2 * cand + number]
            )
            copy.start()
            copies.append(copy)
    for copy in copies:
        copy.wait()


def update(summed, first, second):
    return pl.pallas_call(
        update_kernel,
        in_specs=[LOCAL] * 3,
        out_specs=[FAR] * 2,
        out_shape=[jax.ShapeDtypeStruct(first.shape, F32)] * 2,
        scratch_shapes=[pltpu.VMEM(first.shape, F32)] * 2
        + [pltpu.SemaphoreType.DMA((2 * CANDS,))],
        compiler_params=PARAMS,
        cost_estimate=cost(8 * first.size, 8 * first.size),
        name="update",
    )(summed, first, second)


def backward_kernel(parts, *refs):
    blocks, refs = refs[:parts], refs[parts:]
    w_down, w_gate, w_up, pre_gate, pre_up = refs[:5]
    outs = refs[5:]
    inputs = rows_of([block[...] for block in blocks])
    d_hidden = lax.dot_general(inputs, w_down[...], NT, preferred_element_type=F32)
    gate, up = pre_gate[...], pre_up[...]
    sig = jax.nn.sigmoid(gate)
    d_gate = (d_hidden * up * sig * (1.0 + gate * (1.0 - sig))).astype(BF16)
    d_up = (d_hidden * (gate * sig)).astype(BF16)
    width = w_gate.shape[1]
    step = width // 4
    for piece in range(4):
        at = slice(piece * step, (piece + 1) * step)
        out = jnp.dot(d_gate, w_gate[:, at], preferred_element_type=F32)
        out = out + jnp.dot(d_up, w_up[:, at], preferred_element_type=F32)
        for part in range(parts):
            outs[part][:, at] = out[part * CAP : (part + 1) * CAP, :].astype(BF16)


def backward(blocks, w_down, w_gate, w_up, pre_gate, pre_up):
    units, width = w_down.shape
    parts = len(blocks)
    count = parts * CAP
    return pl.pallas_call(
        functools.partial(backward_kernel, parts),
        in_specs=[LOCAL] * (parts + 5),
        out_specs=[LOCAL] * parts,
        out_shape=[jax.ShapeDtypeStruct((CAP, width), BF16)] * parts,
        compiler_params=PARAMS,
        cost_estimate=cost(6 * count * units * width, 6 * units * width),
        name="backward",
    )(*blocks, w_down, w_gate, w_up, pre_gate, pre_up)


def combine_kernel(parts, pieces, *refs):
    picks, blocks, out, held, sems = refs[0], refs[1 : 1 + parts], *refs[1 + parts :]
    width = out.shape[1]
    step = width // pieces
    left = jnp.where(picks[...] > 0.0, 1.0, 0.0).astype(BF16)
    if left.shape[0] < parts * CAP:
        left = rows_of([left] * parts)
    copies = []
    for piece in range(pieces):
        at = slice(piece * step, (piece + 1) * step)
        rows = rows_of([block[:, at] for block in blocks])
        held[:, at] = lax.dot_general(left, rows, TN, preferred_element_type=F32).astype(BF16)
        copy = pltpu.make_async_copy(held.at[:, at], out.at[:, at], sems.at[piece])
        copy.start()
        copies.append(copy)
    for copy in copies:
        copy.wait()


def combine(picks, blocks):
    count, tok = picks.shape
    width = blocks[0].shape[1]
    pieces = 4
    return pl.pallas_call(
        functools.partial(combine_kernel, len(blocks), pieces),
        in_specs=[LOCAL] * (1 + len(blocks)),
        out_specs=FAR,
        out_shape=jax.ShapeDtypeStruct((tok, width), BF16),
        scratch_shapes=[pltpu.VMEM((tok, width), BF16), pltpu.SemaphoreType.DMA((pieces,))],
        compiler_params=PARAMS,
        cost_estimate=cost(2 * count * tok * width, 2 * tok * width),
        name="combine",
    )(picks, *blocks)


def place_kernel(groups, *refs):
    me = lax.axis_index("grp")
    blocks, out, sems = refs[:groups], refs[groups], refs[groups + 1]
    columns = blocks[0].shape[1]
    copies = []
    for peer in range(groups):
        start = pl.multiple_of((me ^ peer) * columns, 128)
        copies.append(
            pltpu.make_async_copy(
                blocks[peer], out.at[:, pl.ds(start, columns)], sems.at[peer]
            )
        )
        copies[-1].start()
    for copy in copies:
        copy.wait()


def place_blocks(blocks):
    groups = len(blocks)
    units, columns = blocks[0].shape
    return pl.pallas_call(
        functools.partial(place_kernel, groups),
        in_specs=[LOCAL] * groups,
        out_specs=FAR,
        out_shape=jax.ShapeDtypeStruct((units, groups * columns), BF16),
        scratch_shapes=[pltpu.SemaphoreType.DMA((groups,))],
        compiler_params=PARAMS,
        cost_estimate=cost(0, 4 * groups * units * columns),
        name="place_blocks",
    )(*blocks)


def swap(value, axis, size, bits):
    return lax.ppermute(value, axis, [(i, i ^ bits) for i in range(size)])


def body(
    tokens,
    expert_ids,
    gate_probs,
    placement,
    gate_weight,
    up_weight,
    down_weight,
    out_grad,
    moment_first,
    moment_second,
):
    num_ep = lax.axis_size("ep")
    groups = lax.axis_size("grp")
    slots = num_ep // QUARTERS
    ep_index = lax.axis_index("ep")

    def slot_of(bits):
        return (ep_index ^ bits) // QUARTERS

    def of_slot(value, bits, axis):
        if slots == 1:
            return lax.squeeze(value, (axis,))
        return lax.dynamic_index_in_dim(value, slot_of(bits), axis, keepdims=False)

    def share(value, axis):
        got = [None] * num_ep
        for far in range(0, num_ep, 2):
            piece = of_slot(value, far, axis)
            got[far] = swap(piece, "ep", num_ep, far) if far else piece
        for far in range(0, num_ep, 2):
            got[far + 1] = swap(got[far], "ep", num_ep, 1)
        return got

    def exchange(values):
        got = [values[0]]
        for bits in range(1, groups):
            got.append(swap(values[bits], "grp", groups, bits))
        return got

    def per_slot(value):
        return value.reshape((slots, CAP) + value.shape[1:])

    w_gate = gate_weight[0].T
    w_up = up_weight[0].T
    w_down = down_weight[0]

    rows, picks = select(placement, expert_ids.T, gate_probs.T, tokens, slots)
    in_rows = share(per_slot(rows), 0)
    scaled, *blocks = scale(picks, out_grad, groups)
    if slots > 1:
        picks = [of_slot(per_slot(picks), bits, 0) for bits in range(num_ep)]
        picks = jnp.concatenate(picks, axis=0)
    pairs = [blocks[0]]
    for number in range(1, groups // 2):
        pairs.append(swap(blocks[number], "grp", groups, 2 * number))
    kept, passed = stack(pairs)
    passed = swap(passed, "grp", groups, 1)
    columns = join(kept, passed)
    columns = columns.reshape(groups, slots, CAP, columns.shape[-1])
    near = []
    for far in range(0, num_ep, 2):
        piece = of_slot(columns, far, 1)
        near.append(swap(piece, "ep", num_ep, far) if far else piece)
    near = functools.reduce(join, near)
    columns = (near, swap(near, "ep", num_ep, 1))
    my_cand = placement
    if slots > 1:
        my_cand = lax.dynamic_index_in_dim(placement, slot_of(0), 1, keepdims=True)
    pre_gate, pre_up, hidden = forward(my_cand, in_rows, w_gate, w_up)
    hiddens = exchange([hidden] * groups)
    summed, *dirs = adam(hiddens, columns, moment_first, moment_second)
    got_dirs = exchange(dirs)
    new_first, new_second = update(summed, moment_first, moment_second)

    in_scaled = share(per_slot(scaled), 0)
    partials = backward(in_scaled, w_down, w_gate, w_up, pre_gate, pre_up)
    returned = [partials[0]]
    for bits in range(1, num_ep):
        returned.append(swap(partials[bits], "ep", num_ep, bits))
    token_grad = combine(picks, returned)
    step_dir = place_blocks(got_dirs)[None]
    return (token_grad, step_dir, new_first, new_second)


def solution(mesh):
    return jax.shard_map(
        body,
        mesh=mesh,
        in_specs=(
            P(("grp", "ep"), None),
            P(("grp", "ep"), None),
            P(("grp", "ep"), None),
            P("grp", None),
            P("grp", None, "ep"),
            P("grp", None, "ep"),
            P("grp", "ep", None),
            P(("grp", "ep"), None),
            P(None, "ep", "grp"),
            P(None, "ep", "grp"),
        ),
        out_specs=(
            P(("grp", "ep"), None),
            P("grp", "ep", None),
            P(None, "ep", "grp"),
            P(None, "ep", "grp"),
        ),
        check_vma=False,
    )
```

```python
import functools
import math

import jax
import jax.numpy as jnp
from jax import lax
from jax.experimental import pallas as pl
from jax.experimental.pallas import tpu as pltpu
from jax.sharding import PartitionSpec as P


QUARTERS = 4
CANDS = 2
CAP = 24
TAG = 16


beta_one = 0.9
beta_two = 0.999
adam_eps = 1e-08
first_fix = 1.0 - math.exp(1000.0 * math.log(0.9))
second_fix = 1.0 - math.exp(1000.0 * math.log(0.999))

F32 = jnp.float32
BF16 = jnp.bfloat16
NT = (((1,), (1,)), ((), ()))
TN = (((0,), (0,)), ((), ()))


SCALARS = pl.BlockSpec(memory_space=pltpu.SMEM)
LOCAL = pl.BlockSpec(memory_space=pltpu.VMEM)
FAR = pl.BlockSpec(memory_space=pltpu.HBM)
PARAMS = pltpu.CompilerParams(vmem_limit_bytes=12 * 2**20)
GRANT1 = pltpu.CompilerParams(vmem_limit_bytes=65_400_000)
GRANT2 = pltpu.CompilerParams(vmem_limit_bytes=56_000_000)


def cost(flops, moved):
    return pl.CostEstimate(flops=int(flops), bytes_accessed=int(moved) * 16, transcendentals=0)


def rows_of(parts):
    return jnp.concatenate([part.astype(F32) for part in parts], axis=0).astype(BF16)


def select_kernel(slots, pieces, place, ids, probs, tokens, rows, picks, *refs):
    ids_in, probs_in, tokens_in, sems = refs
    tok, width = tokens.shape
    step = width // pieces
    at = [slice(piece * step, (piece + 1) * step) for piece in range(pieces)]
    pairs = [(ids, ids_in), (probs, probs_in)]
    pairs += [(tokens.at[:, at[i]], tokens_in.at[:, at[i]]) for i in range(pieces)]
    copies = []
    for number, (source, target) in enumerate(pairs):
        copies.append(pltpu.make_async_copy(source, target, sems.at[number]))
        copies[-1].start()
    below = lax.broadcasted_iota(jnp.int32, (tok, tok), 0)
    right = lax.broadcasted_iota(jnp.int32, (tok, tok), 1)
    upper = jnp.where(below <= right, 1.0, 0.0).astype(BF16)
    want = lax.broadcasted_iota(jnp.int32, (CAP, tok), 0).astype(F32) + 1.0
    for copy in copies[:2]:
        copy.wait()
    chosen_list = []
    for slot in range(slots):
        expert = place[0, slot] * slots + slot
        match = ids_in[...] == expert
        hit = jnp.max(jnp.where(match, 1.0, 0.0), axis=0, keepdims=True)
        coef = jnp.sum(jnp.where(match, probs_in[...], 0.0), axis=0, keepdims=True)
        rank = jnp.dot(hit.astype(BF16), upper, preferred_element_type=F32)
        chosen = jnp.where((rank == want) & (hit > 0.0), 1.0, 0.0)
        chosen_list.append(chosen)
        picks[slot * CAP : (slot + 1) * CAP, :] = chosen * coef
    left = jnp.concatenate(chosen_list, axis=0) if slots > 1 else chosen_list[0]
    left = left.astype(BF16)
    for i in range(pieces):
        copies[2 + i].wait()
        picked = jnp.dot(left, tokens_in[:, at[i]], preferred_element_type=F32)
        rows[:, at[i]] = picked.astype(BF16)


def select(placement, ids, probs, tokens, slots):
    tok, width = tokens.shape
    pieces = 4
    count = slots * CAP
    return pl.pallas_call(
        functools.partial(select_kernel, slots, pieces),
        in_specs=[SCALARS] + [FAR] * 3,
        out_specs=[LOCAL] * 2,
        out_shape=[
            jax.ShapeDtypeStruct((count, width), BF16),
            jax.ShapeDtypeStruct((count, tok), F32),
        ],
        scratch_shapes=[
            pltpu.VMEM(ids.shape, ids.dtype),
            pltpu.VMEM(probs.shape, probs.dtype),
            pltpu.VMEM((tok, width), BF16),
            pltpu.SemaphoreType.DMA((2 + pieces,)),
        ],
        compiler_params=GRANT1,
        cost_estimate=cost(2 * count * tok * width, tok * width * 2),
        name="select_rows",
    )(placement, ids, probs, tokens)


def scale_kernel(pieces, picks, grads, scaled, *refs):
    me = lax.axis_index("grp")
    blocks, (grads_in, sems) = refs[:-2], refs[-2:]
    groups = 2 * len(blocks)
    width = grads.shape[1]
    block, step = width // groups, width // pieces
    at = [slice(piece * step, (piece + 1) * step) for piece in range(pieces)]
    copies = []
    for i in range(pieces):
        copies.append(
            pltpu.make_async_copy(grads.at[:, at[i]], grads_in.at[:, at[i]], sems.at[i])
        )
        copies[-1].start()
    coefs = jnp.sum(picks[...], axis=1, keepdims=True)
    left = jnp.where(picks[...] > 0.0, 1.0, 0.0).astype(BF16)
    for i in range(pieces):
        copies[i].wait()
        picked = jnp.dot(left, grads_in[:, at[i]], preferred_element_type=F32)
        scaled[:, at[i]] = (coefs * picked).astype(BF16)
    for group in range(groups):
        start = pl.multiple_of((me ^ group) * block, 128)
        blocks[group // 2][group % 2] = scaled[:, pl.ds(start, block)]


def scale(picks, grads, groups):
    tok, width = grads.shape
    pieces = 4
    count = picks.shape[0]
    pairs = groups // 2
    return pl.pallas_call(
        functools.partial(scale_kernel, pieces),
        in_specs=[LOCAL, FAR],
        out_specs=[LOCAL] * (1 + pairs),
        out_shape=[jax.ShapeDtypeStruct((count, width), BF16)]
        + [jax.ShapeDtypeStruct((2, count, width // groups), BF16)] * pairs,
        scratch_shapes=[pltpu.VMEM((tok, width), BF16), pltpu.SemaphoreType.DMA((pieces,))],
        compiler_params=GRANT2,
        cost_estimate=cost(2 * count * tok * width, tok * width * 8),
        name="scale_rows",
    )(picks, grads)


def stack_kernel(count, *refs):
    for number in range(count):
        for pick, out in enumerate(refs[count:]):
            out[number] = refs[number][pick]


def stack(pairs):
    shape = (len(pairs),) + pairs[0].shape[1:]
    return pl.pallas_call(
        functools.partial(stack_kernel, len(pairs)),
        in_specs=[LOCAL] * len(pairs),
        out_specs=[LOCAL] * 2,
        out_shape=[jax.ShapeDtypeStruct(shape, BF16)] * 2,
        compiler_params=PARAMS,
        cost_estimate=cost(0, 2 * len(pairs) * pairs[0].size),
        name="stack",
    )(*pairs)


def join_kernel(one, two, out):
    count = one.shape[0]
    out[0:count] = one[...]
    out[count:] = two[...]


def join(one, two):
    shape = (one.shape[0] + two.shape[0],) + one.shape[1:]
    return pl.pallas_call(
        join_kernel,
        in_specs=[LOCAL] * 2,
        out_specs=LOCAL,
        out_shape=jax.ShapeDtypeStruct(shape, BF16),
        compiler_params=PARAMS,
        cost_estimate=cost(0, 8 * one.size),
        name="join",
    )(one, two)


def forward_kernel(parts, place, *refs):
    blocks, (w_gate, w_up, pre_gate, pre_up, hidden) = refs[:parts], refs[parts:]
    inputs = rows_of([block[...] for block in blocks])
    gate = lax.dot_general(inputs, w_gate[...], NT, preferred_element_type=F32)
    up = lax.dot_general(inputs, w_up[...], NT, preferred_element_type=F32)
    pre_gate[...] = gate
    pre_up[...] = up
    count = gate.shape[0]
    hidden[0:count, :] = (gate * jax.nn.sigmoid(gate) * up).astype(BF16)
    tag = place[0, 0].astype(F32)
    hidden[count : count + TAG, :] = jnp.full((TAG, gate.shape[1]), tag, F32).astype(BF16)


def forward(my_cand, blocks, w_gate, w_up):
    units, width = w_gate.shape
    count = len(blocks) * CAP
    return pl.pallas_call(
        functools.partial(forward_kernel, len(blocks)),
        in_specs=[SCALARS] + [LOCAL] * (len(blocks) + 2),
        out_specs=[LOCAL] * 3,
        out_shape=[
            jax.ShapeDtypeStruct((count, units), F32),
            jax.ShapeDtypeStruct((count, units), F32),
            jax.ShapeDtypeStruct((count + TAG, units), BF16),
        ],
        compiler_params=PARAMS,
        cost_estimate=cost(4 * count * units * width, 4 * units * width),
        name="forward",
    )(my_cand, *blocks, w_gate, w_up)


def adam_kernel(groups, parts, *refs):
    half = groups // 2
    hiddens, refs = refs[:groups], refs[groups:]
    near, other, first, second, summed = refs[:5]
    dirs = refs[5:]
    count = parts * CAP
    rights = []
    lefts = [[] for _ in range(CANDS)]
    for peer in range(groups):
        held = hiddens[peer]
        part_rows = held[0:count, :].astype(F32)
        tag = held[count : count + TAG, :].astype(F32)[0:1, :]
        for cand in range(CANDS):
            lefts[cand].append(jnp.where(tag == float(cand), part_rows, 0.0))
        for part in range(parts):
            stack = (near, other)[part % 2]
            at = part // 2 * groups + peer // 2 + peer % 2 * half
            rights.append(stack[at].astype(F32))
    right = jnp.concatenate(rights, axis=0).astype(BF16)
    dir_list = []
    for cand in range(CANDS):
        left = jnp.concatenate(lefts[cand], axis=0).astype(BF16)
        grad = lax.dot_general(left, right, TN, preferred_element_type=F32)
        summed[cand] = grad
        one, two = moments(grad, first[cand], second[cand])
        dir_list.append(one / first_fix / (jnp.sqrt(two / second_fix) + adam_eps))
    both = dirs[groups]
    split = dir_list[0].shape[0] - both.shape[1]
    for cand in range(CANDS):
        both[cand] = dir_list[cand][split:].astype(BF16)
    for peer in range(groups):
        tag = hiddens[peer][count : count + TAG, :].astype(F32)[0:1, 0:1]
        out = dir_list[0]
        for cand in range(1, CANDS):
            out = jnp.where(tag == float(cand), dir_list[cand], out)
        dirs[peer][...] = out[: dirs[peer].shape[0]].astype(BF16)


def moments(gradient, first_moment, second):
    new_first = beta_one * first_moment + (1.0 - beta_one) * gradient
    new_second = beta_two * second + (1.0 - beta_two) * gradient * gradient
    return (new_first, new_second)


def adam(hiddens, blocks, first, second):
    groups = len(hiddens)
    parts = 2 * blocks[0].shape[0] // groups
    units, columns = first.shape[1:]
    split = units // 2
    rows = groups * parts * CAP
    return pl.pallas_call(
        functools.partial(adam_kernel, groups, parts),
        in_specs=[LOCAL] * (groups + 4),
        out_specs=[LOCAL] * (2 + groups),
        out_shape=[jax.ShapeDtypeStruct(first.shape, F32)]
        + [jax.ShapeDtypeStruct((units, columns), BF16)] * (groups // 2)
        + [jax.ShapeDtypeStruct((split, columns), BF16)] * (groups // 2)
        + [jax.ShapeDtypeStruct((CANDS, units - split, columns), BF16)],
        compiler_params=PARAMS,
        cost_estimate=cost(2 * CANDS * rows * units * columns, 8 * first.size),
        name="adam",
    )(*hiddens, *blocks, first, second)


def choose_kernel(half, *refs):
    hiddens, both, outs = refs[:half], refs[half], refs[half + 1 :]
    for peer in range(half):
        count = hiddens[peer].shape[0] - TAG
        tag = hiddens[peer][count : count + TAG, :].astype(F32)[0:1, 0:1]
        out = both[0].astype(F32)
        for cand in range(1, CANDS):
            out = jnp.where(tag == float(cand), both[cand].astype(F32), out)
        outs[peer][...] = out.astype(BF16)


def choose(hiddens, both):
    half = len(hiddens)
    return pl.pallas_call(
        functools.partial(choose_kernel, half),
        in_specs=[LOCAL] * (half + 1),
        out_specs=[LOCAL] * half,
        out_shape=[jax.ShapeDtypeStruct(both.shape[1:], BF16)] * half,
        compiler_params=PARAMS,
        cost_estimate=cost(both.size, 2 * half * both.size),
        name="choose",
    )(*hiddens, both)


def update_kernel(summed, first, second, new_first, new_second, one_out, two_out, sems):
    copies = []
    for cand in range(CANDS):
        one_out[cand], two_out[cand] = moments(summed[cand], first[cand], second[cand])
        for number, (source, target) in enumerate([(one_out, new_first), (two_out, new_second)]):
            copy = pltpu.make_async_copy(
                source.at[cand], target.at[cand], sems.at[2 * cand + number]
            )
            copy.start()
            copies.append(copy)
    for copy in copies:
        copy.wait()


def update(summed, first, second):
    return pl.pallas_call(
        update_kernel,
        in_specs=[LOCAL] * 3,
        out_specs=[FAR] * 2,
        out_shape=[jax.ShapeDtypeStruct(first.shape, F32)] * 2,
        scratch_shapes=[pltpu.VMEM(first.shape, F32)] * 2
        + [pltpu.SemaphoreType.DMA((2 * CANDS,))],
        compiler_params=PARAMS,
        cost_estimate=cost(8 * first.size, 8 * first.size),
        name="update",
    )(summed, first, second)


def backward_kernel(parts, *refs):
    blocks, refs = refs[:parts], refs[parts:]
    w_down, w_gate, w_up, pre_gate, pre_up = refs[:5]
    outs = refs[5:]
    inputs = rows_of([block[...] for block in blocks])
    d_hidden = lax.dot_general(inputs, w_down[...], NT, preferred_element_type=F32)
    gate, up = pre_gate[...], pre_up[...]
    sig = jax.nn.sigmoid(gate)
    d_gate = (d_hidden * up * sig * (1.0 + gate * (1.0 - sig))).astype(BF16)
    d_up = (d_hidden * (gate * sig)).astype(BF16)
    width = w_gate.shape[1]
    step = width // 4
    for piece in range(4):
        at = slice(piece * step, (piece + 1) * step)
        out = jnp.dot(d_gate, w_gate[:, at], preferred_element_type=F32)
        out = out + jnp.dot(d_up, w_up[:, at], preferred_element_type=F32)
        for part in range(parts):
            outs[part][:, at] = out[part * CAP : (part + 1) * CAP, :].astype(BF16)


def backward(blocks, w_down, w_gate, w_up, pre_gate, pre_up):
    units, width = w_down.shape
    parts = len(blocks)
    count = parts * CAP
    return pl.pallas_call(
        functools.partial(backward_kernel, parts),
        in_specs=[LOCAL] * (parts + 5),
        out_specs=[LOCAL] * parts,
        out_shape=[jax.ShapeDtypeStruct((CAP, width), BF16)] * parts,
        compiler_params=PARAMS,
        cost_estimate=cost(6 * count * units * width, 6 * units * width),
        name="backward",
    )(*blocks, w_down, w_gate, w_up, pre_gate, pre_up)


def combine_kernel(parts, pieces, *refs):
    picks, blocks, out, held, sems = refs[0], refs[1 : 1 + parts], *refs[1 + parts :]
    width = out.shape[1]
    step = width // pieces
    left = jnp.where(picks[...] > 0.0, 1.0, 0.0).astype(BF16)
    if left.shape[0] < parts * CAP:
        left = rows_of([left] * parts)
    copies = []
    for piece in range(pieces):
        at = slice(piece * step, (piece + 1) * step)
        rows = rows_of([block[:, at] for block in blocks])
        held[:, at] = lax.dot_general(left, rows, TN, preferred_element_type=F32).astype(BF16)
        copy = pltpu.make_async_copy(held.at[:, at], out.at[:, at], sems.at[piece])
        copy.start()
        copies.append(copy)
    for copy in copies:
        copy.wait()


def combine(picks, blocks):
    count, tok = picks.shape
    width = blocks[0].shape[1]
    pieces = 4
    return pl.pallas_call(
        functools.partial(combine_kernel, len(blocks), pieces),
        in_specs=[LOCAL] * (1 + len(blocks)),
        out_specs=FAR,
        out_shape=jax.ShapeDtypeStruct((tok, width), BF16),
        scratch_shapes=[pltpu.VMEM((tok, width), BF16), pltpu.SemaphoreType.DMA((pieces,))],
        compiler_params=PARAMS,
        cost_estimate=cost(2 * count * tok * width, 2 * tok * width),
        name="combine",
    )(picks, *blocks)


def place_kernel(groups, *refs):
    me = lax.axis_index("grp")
    half = groups // 2
    blocks, (out, sems) = refs[: groups + half], refs[groups + half :]
    units, columns = blocks[0].shape
    copies = []
    for number, block in enumerate(blocks):
        rows = block.shape[0]
        peer = number if number < groups else number - half
        start = pl.multiple_of((me ^ peer) * columns, 128)
        at = pl.ds(0 if number < groups else units - rows, rows)
        target = out.at[at, pl.ds(start, columns)]
        copies.append(pltpu.make_async_copy(block, target, sems.at[number]))
        copies[-1].start()
    for copy in copies:
        copy.wait()


def place_blocks(groups, blocks):
    units, columns = blocks[0].shape
    return pl.pallas_call(
        functools.partial(place_kernel, groups),
        in_specs=[LOCAL] * len(blocks),
        out_specs=FAR,
        out_shape=jax.ShapeDtypeStruct((units, groups * columns), BF16),
        scratch_shapes=[pltpu.SemaphoreType.DMA((len(blocks),))],
        compiler_params=PARAMS,
        cost_estimate=cost(0, 4 * groups * units * columns),
        name="place_blocks",
    )(*blocks)


def swap(value, axis, size, bits):
    return lax.ppermute(value, axis, [(i, i ^ bits) for i in range(size)])


def body(
    tokens,
    expert_ids,
    gate_probs,
    placement,
    gate_weight,
    up_weight,
    down_weight,
    out_grad,
    moment_first,
    moment_second,
):
    num_ep = lax.axis_size("ep")
    groups = lax.axis_size("grp")
    slots = num_ep // QUARTERS
    ep_index = lax.axis_index("ep")

    def slot_of(bits):
        return (ep_index ^ bits) // QUARTERS

    def of_slot(value, bits, axis):
        if slots == 1:
            return lax.squeeze(value, (axis,))
        return lax.dynamic_index_in_dim(value, slot_of(bits), axis, keepdims=False)

    def share(value, axis):
        got = [None] * num_ep
        for far in range(0, num_ep, 2):
            piece = of_slot(value, far, axis)
            got[far] = swap(piece, "ep", num_ep, far) if far else piece
        for far in range(0, num_ep, 2):
            got[far + 1] = swap(got[far], "ep", num_ep, 1)
        return got

    def exchange(values):
        got = [values[0]]
        for bits in range(1, len(values)):
            got.append(swap(values[bits], "grp", groups, bits))
        return got

    def per_slot(value):
        return value.reshape((slots, CAP) + value.shape[1:])

    w_gate = gate_weight[0].T
    w_up = up_weight[0].T
    w_down = down_weight[0]

    rows, picks = select(placement, expert_ids.T, gate_probs.T, tokens, slots)
    in_rows = share(per_slot(rows), 0)
    scaled, *blocks = scale(picks, out_grad, groups)
    if slots > 1:
        picks = [of_slot(per_slot(picks), bits, 0) for bits in range(num_ep)]
        picks = jnp.concatenate(picks, axis=0)
    pairs = [blocks[0]]
    for number in range(1, groups // 2):
        pairs.append(swap(blocks[number], "grp", groups, 2 * number))
    kept, passed = stack(pairs)
    passed = swap(passed, "grp", groups, 1)
    columns = join(kept, passed)
    columns = columns.reshape(groups, slots, CAP, columns.shape[-1])
    near = []
    for far in range(0, num_ep, 2):
        piece = of_slot(columns, far, 1)
        near.append(swap(piece, "ep", num_ep, far) if far else piece)
    near = functools.reduce(join, near)
    columns = (near, swap(near, "ep", num_ep, 1))
    my_cand = placement
    if slots > 1:
        my_cand = lax.dynamic_index_in_dim(placement, slot_of(0), 1, keepdims=True)
    pre_gate, pre_up, hidden = forward(my_cand, in_rows, w_gate, w_up)
    hiddens = exchange([hidden] * groups)
    summed, *dirs, both = adam(hiddens, columns, moment_first, moment_second)
    got_dirs = exchange(dirs)
    both = swap(both, "grp", groups, groups // 2)
    dirs = choose(hiddens[: groups // 2], both)
    got_dirs = got_dirs + exchange(dirs)
    new_first, new_second = update(summed, moment_first, moment_second)

    in_scaled = share(per_slot(scaled), 0)
    partials = backward(in_scaled, w_down, w_gate, w_up, pre_gate, pre_up)
    returned = [partials[0]]
    for bits in range(1, num_ep):
        returned.append(swap(partials[bits], "ep", num_ep, bits))
    token_grad = combine(picks, returned)
    step_dir = place_blocks(groups, got_dirs)[None]
    return (token_grad, step_dir, new_first, new_second)


def solution(mesh):
    return jax.shard_map(
        body,
        mesh=mesh,
        in_specs=(
            P(("grp", "ep"), None),
            P(("grp", "ep"), None),
            P(("grp", "ep"), None),
            P("grp", None),
            P("grp", None, "ep"),
            P("grp", None, "ep"),
            P("grp", "ep", None),
            P(("grp", "ep"), None),
            P(None, "ep", "grp"),
            P(None, "ep", "grp"),
        ),
        out_specs=(
            P(("grp", "ep"), None),
            P("grp", "ep", None),
            P(None, "ep", "grp"),
            P(None, "ep", "grp"),
        ),
        check_vma=False,
    )
```

```python
import functools
import math

import jax
import jax.numpy as jnp
from jax import lax
from jax.experimental import pallas as pl
from jax.experimental.pallas import tpu as pltpu
from jax.sharding import PartitionSpec as P


QUARTERS = 4
CANDS = 2
CAP = 24
TAG = 16


beta_one = 0.9
beta_two = 0.999
adam_eps = 1e-08
first_fix = 1.0 - math.exp(1000.0 * math.log(0.9))
second_fix = 1.0 - math.exp(1000.0 * math.log(0.999))

F32 = jnp.float32
BF16 = jnp.bfloat16
NT = (((1,), (1,)), ((), ()))
TN = (((0,), (0,)), ((), ()))


SCALARS = pl.BlockSpec(memory_space=pltpu.SMEM)
LOCAL = pl.BlockSpec(memory_space=pltpu.VMEM)
FAR = pl.BlockSpec(memory_space=pltpu.HBM)
PARAMS = pltpu.CompilerParams(vmem_limit_bytes=12 * 2**20)
GRANT1 = pltpu.CompilerParams(vmem_limit_bytes=65_400_000)
GRANT2 = pltpu.CompilerParams(vmem_limit_bytes=56_000_000)


def cost(flops, moved):
    return pl.CostEstimate(flops=int(flops), bytes_accessed=int(moved) * 16, transcendentals=0)


def rows_of(parts):
    return jnp.concatenate([part.astype(F32) for part in parts], axis=0).astype(BF16)


def select_kernel(slots, pieces, place, ids, probs, tokens, rows, picks, *refs):
    ids_in, probs_in, tokens_in, sems = refs
    tok, width = tokens.shape
    step = width // pieces
    at = [slice(piece * step, (piece + 1) * step) for piece in range(pieces)]
    pairs = [(ids, ids_in), (probs, probs_in)]
    pairs += [(tokens.at[:, at[i]], tokens_in.at[:, at[i]]) for i in range(pieces)]
    copies = []
    for number, (source, target) in enumerate(pairs):
        copies.append(pltpu.make_async_copy(source, target, sems.at[number]))
        copies[-1].start()
    below = lax.broadcasted_iota(jnp.int32, (tok, tok), 0)
    right = lax.broadcasted_iota(jnp.int32, (tok, tok), 1)
    upper = jnp.where(below <= right, 1.0, 0.0).astype(BF16)
    want = lax.broadcasted_iota(jnp.int32, (CAP, tok), 0).astype(F32) + 1.0
    for copy in copies[:2]:
        copy.wait()
    chosen_list = []
    for slot in range(slots):
        expert = place[0, slot] * slots + slot
        match = ids_in[...] == expert
        hit = jnp.max(jnp.where(match, 1.0, 0.0), axis=0, keepdims=True)
        coef = jnp.sum(jnp.where(match, probs_in[...], 0.0), axis=0, keepdims=True)
        rank = jnp.dot(hit.astype(BF16), upper, preferred_element_type=F32)
        chosen = jnp.where((rank == want) & (hit > 0.0), 1.0, 0.0)
        chosen_list.append(chosen)
        picks[slot * CAP : (slot + 1) * CAP, :] = chosen * coef
    left = jnp.concatenate(chosen_list, axis=0) if slots > 1 else chosen_list[0]
    left = left.astype(BF16)
    for i in range(pieces):
        copies[2 + i].wait()
        picked = jnp.dot(left, tokens_in[:, at[i]], preferred_element_type=F32)
        rows[:, at[i]] = picked.astype(BF16)


def select(placement, ids, probs, tokens, slots):
    tok, width = tokens.shape
    pieces = 4
    count = slots * CAP
    return pl.pallas_call(
        functools.partial(select_kernel, slots, pieces),
        in_specs=[SCALARS] + [FAR] * 3,
        out_specs=[LOCAL] * 2,
        out_shape=[
            jax.ShapeDtypeStruct((count, width), BF16),
            jax.ShapeDtypeStruct((count, tok), F32),
        ],
        scratch_shapes=[
            pltpu.VMEM(ids.shape, ids.dtype),
            pltpu.VMEM(probs.shape, probs.dtype),
            pltpu.VMEM((tok, width), BF16),
            pltpu.SemaphoreType.DMA((2 + pieces,)),
        ],
        compiler_params=GRANT1,
        cost_estimate=cost(2 * count * tok * width, tok * width * 2),
        name="select_rows",
    )(placement, ids, probs, tokens)


def scale_kernel(pieces, picks, grads, scaled, *refs):
    me = lax.axis_index("grp")
    blocks, (grads_in, sems) = refs[:-2], refs[-2:]
    groups = 2 * len(blocks)
    width = grads.shape[1]
    block, step = width // groups, width // pieces
    at = [slice(piece * step, (piece + 1) * step) for piece in range(pieces)]
    copies = []
    for i in range(pieces):
        copies.append(
            pltpu.make_async_copy(grads.at[:, at[i]], grads_in.at[:, at[i]], sems.at[i])
        )
        copies[-1].start()
    coefs = jnp.sum(picks[...], axis=1, keepdims=True)
    left = jnp.where(picks[...] > 0.0, 1.0, 0.0).astype(BF16)
    for i in range(pieces):
        copies[i].wait()
        picked = jnp.dot(left, grads_in[:, at[i]], preferred_element_type=F32)
        scaled[:, at[i]] = (coefs * picked).astype(BF16)
    for group in range(groups):
        start = pl.multiple_of((me ^ group) * block, 128)
        blocks[group // 2][group % 2] = scaled[:, pl.ds(start, block)]


def scale(picks, grads, groups):
    tok, width = grads.shape
    pieces = 4
    count = picks.shape[0]
    pairs = groups // 2
    return pl.pallas_call(
        functools.partial(scale_kernel, pieces),
        in_specs=[LOCAL, FAR],
        out_specs=[LOCAL] * (1 + pairs),
        out_shape=[jax.ShapeDtypeStruct((count, width), BF16)]
        + [jax.ShapeDtypeStruct((2, count, width // groups), BF16)] * pairs,
        scratch_shapes=[pltpu.VMEM((tok, width), BF16), pltpu.SemaphoreType.DMA((pieces,))],
        compiler_params=GRANT2,
        cost_estimate=cost(2 * count * tok * width, tok * width * 8),
        name="scale_rows",
    )(picks, grads)


def stack_kernel(count, *refs):
    for number in range(count):
        for pick, out in enumerate(refs[count:]):
            out[number] = refs[number][pick]


def stack(pairs):
    shape = (len(pairs),) + pairs[0].shape[1:]
    return pl.pallas_call(
        functools.partial(stack_kernel, len(pairs)),
        in_specs=[LOCAL] * len(pairs),
        out_specs=[LOCAL] * 2,
        out_shape=[jax.ShapeDtypeStruct(shape, BF16)] * 2,
        compiler_params=PARAMS,
        cost_estimate=cost(0, 2 * len(pairs) * pairs[0].size),
        name="stack",
    )(*pairs)


def pile_kernel(count, *refs):
    for number in range(count):
        refs[count][number] = refs[number][...]


def pile(blocks):
    return pl.pallas_call(
        functools.partial(pile_kernel, len(blocks)),
        in_specs=[LOCAL] * len(blocks),
        out_specs=LOCAL,
        out_shape=jax.ShapeDtypeStruct((len(blocks),) + blocks[0].shape, BF16),
        compiler_params=PARAMS,
        cost_estimate=cost(0, 4 * len(blocks) * blocks[0].size),
        name="pile",
    )(*blocks)


def join_kernel(one, two, out):
    count = one.shape[0]
    out[0:count] = one[...]
    out[count:] = two[...]


def join(one, two):
    shape = (one.shape[0] + two.shape[0],) + one.shape[1:]
    return pl.pallas_call(
        join_kernel,
        in_specs=[LOCAL] * 2,
        out_specs=LOCAL,
        out_shape=jax.ShapeDtypeStruct(shape, BF16),
        compiler_params=PARAMS,
        cost_estimate=cost(0, 8 * one.size),
        name="join",
    )(one, two)


def forward_kernel(parts, place, *refs):
    blocks, (w_gate, w_up, pre_gate, pre_up, hidden) = refs[:parts], refs[parts:]
    inputs = rows_of([block[...] for block in blocks])
    gate = lax.dot_general(inputs, w_gate[...], NT, preferred_element_type=F32)
    up = lax.dot_general(inputs, w_up[...], NT, preferred_element_type=F32)
    pre_gate[...] = gate
    pre_up[...] = up
    count = gate.shape[0]
    hidden[0:count, :] = (gate * jax.nn.sigmoid(gate) * up).astype(BF16)
    tag = place[0, 0].astype(F32)
    hidden[count : count + TAG, :] = jnp.full((TAG, gate.shape[1]), tag, F32).astype(BF16)


def forward(my_cand, blocks, w_gate, w_up):
    units, width = w_gate.shape
    count = len(blocks) * CAP
    return pl.pallas_call(
        functools.partial(forward_kernel, len(blocks)),
        in_specs=[SCALARS] + [LOCAL] * (len(blocks) + 2),
        out_specs=[LOCAL] * 3,
        out_shape=[
            jax.ShapeDtypeStruct((count, units), F32),
            jax.ShapeDtypeStruct((count, units), F32),
            jax.ShapeDtypeStruct((count + TAG, units), BF16),
        ],
        compiler_params=PARAMS,
        cost_estimate=cost(4 * count * units * width, 4 * units * width),
        name="forward",
    )(my_cand, *blocks, w_gate, w_up)


def adam_kernel(groups, parts, *refs):
    half = groups // 2
    hiddens, refs = [refs[p % 2].at[p // 2] for p in range(groups)], refs[2:]
    near, other, first, second, summed = refs[:5]
    dirs = refs[5:]
    count = parts * CAP
    rights = []
    lefts = [[] for _ in range(CANDS)]
    for peer in range(groups):
        held = hiddens[peer]
        part_rows = held[0:count, :].astype(F32)
        tag = held[count : count + TAG, :].astype(F32)[0:1, :]
        for cand in range(CANDS):
            lefts[cand].append(jnp.where(tag == float(cand), part_rows, 0.0))
        for part in range(parts):
            stack = (near, other)[part % 2]
            at = part // 2 * groups + peer // 2 + peer % 2 * half
            rights.append(stack[at].astype(F32))
    right = jnp.concatenate(rights, axis=0).astype(BF16)
    dir_list = []
    for cand in range(CANDS):
        left = jnp.concatenate(lefts[cand], axis=0).astype(BF16)
        grad = lax.dot_general(left, right, TN, preferred_element_type=F32)
        summed[cand] = grad
        one, two = moments(grad, first[cand], second[cand])
        dir_list.append(one / first_fix / (jnp.sqrt(two / second_fix) + adam_eps))
    both = dirs[groups]
    split = dir_list[0].shape[0] - both.shape[1]
    for cand in range(CANDS):
        both[cand] = dir_list[cand][split:].astype(BF16)
    for peer in range(groups):
        tag = hiddens[peer][count : count + TAG, :].astype(F32)[0:1, 0:1]
        out = dir_list[0]
        for cand in range(1, CANDS):
            out = jnp.where(tag == float(cand), dir_list[cand], out)
        dirs[peer][...] = out[: dirs[peer].shape[0]].astype(BF16)


def moments(gradient, first_moment, second):
    new_first = beta_one * first_moment + (1.0 - beta_one) * gradient
    new_second = beta_two * second + (1.0 - beta_two) * gradient * gradient
    return (new_first, new_second)


def adam(hiddens, blocks, first, second):
    groups = 2 * hiddens[0].shape[0]
    parts = 2 * blocks[0].shape[0] // groups
    units, columns = first.shape[1:]
    split = units // 2
    rows = groups * parts * CAP
    return pl.pallas_call(
        functools.partial(adam_kernel, groups, parts),
        in_specs=[LOCAL] * 6,
        out_specs=[LOCAL] * (2 + groups),
        out_shape=[jax.ShapeDtypeStruct(first.shape, F32)]
        + [jax.ShapeDtypeStruct((units, columns), BF16)] * (groups // 2)
        + [jax.ShapeDtypeStruct((split, columns), BF16)] * (groups // 2)
        + [jax.ShapeDtypeStruct((CANDS, units - split, columns), BF16)],
        compiler_params=PARAMS,
        cost_estimate=cost(2 * CANDS * rows * units * columns, 8 * first.size),
        name="adam",
    )(*hiddens, *blocks, first, second)


def choose_kernel(half, *refs):
    hiddens, both, outs = [refs[p % 2].at[p // 2] for p in range(half)], refs[2], refs[3:]
    for peer in range(half):
        count = hiddens[peer].shape[0] - TAG
        tag = hiddens[peer][count : count + TAG, :].astype(F32)[0:1, 0:1]
        out = both[0].astype(F32)
        for cand in range(1, CANDS):
            out = jnp.where(tag == float(cand), both[cand].astype(F32), out)
        outs[peer][...] = out.astype(BF16)


def choose(hiddens, both):
    half = hiddens[0].shape[0]
    return pl.pallas_call(
        functools.partial(choose_kernel, half),
        in_specs=[LOCAL] * 3,
        out_specs=[LOCAL] * half,
        out_shape=[jax.ShapeDtypeStruct(both.shape[1:], BF16)] * half,
        compiler_params=PARAMS,
        cost_estimate=cost(both.size, 2 * half * both.size),
        name="choose",
    )(*hiddens, both)


def update_kernel(summed, first, second, new_first, new_second, one_out, two_out, sems):
    copies = []
    for cand in range(CANDS):
        one_out[cand], two_out[cand] = moments(summed[cand], first[cand], second[cand])
        for number, (source, target) in enumerate([(one_out, new_first), (two_out, new_second)]):
            copy = pltpu.make_async_copy(
                source.at[cand], target.at[cand], sems.at[2 * cand + number]
            )
            copy.start()
            copies.append(copy)
    for copy in copies:
        copy.wait()


def update(summed, first, second):
    return pl.pallas_call(
        update_kernel,
        in_specs=[LOCAL] * 3,
        out_specs=[FAR] * 2,
        out_shape=[jax.ShapeDtypeStruct(first.shape, F32)] * 2,
        scratch_shapes=[pltpu.VMEM(first.shape, F32)] * 2
        + [pltpu.SemaphoreType.DMA((2 * CANDS,))],
        compiler_params=PARAMS,
        cost_estimate=cost(8 * first.size, 8 * first.size),
        name="update",
    )(summed, first, second)


def backward_kernel(parts, *refs):
    blocks, refs = refs[:parts], refs[parts:]
    w_down, w_gate, w_up, pre_gate, pre_up = refs[:5]
    outs = refs[5:]
    inputs = rows_of([block[...] for block in blocks])
    d_hidden = lax.dot_general(inputs, w_down[...], NT, preferred_element_type=F32)
    gate, up = pre_gate[...], pre_up[...]
    sig = jax.nn.sigmoid(gate)
    d_gate = (d_hidden * up * sig * (1.0 + gate * (1.0 - sig))).astype(BF16)
    d_up = (d_hidden * (gate * sig)).astype(BF16)
    width = w_gate.shape[1]
    step = width // 4
    for piece in range(4):
        at = slice(piece * step, (piece + 1) * step)
        out = jnp.dot(d_gate, w_gate[:, at], preferred_element_type=F32)
        out = out + jnp.dot(d_up, w_up[:, at], preferred_element_type=F32)
        for part in range(parts):
            outs[part][:, at] = out[part * CAP : (part + 1) * CAP, :].astype(BF16)


def backward(blocks, w_down, w_gate, w_up, pre_gate, pre_up):
    units, width = w_down.shape
    parts = len(blocks)
    count = parts * CAP
    return pl.pallas_call(
        functools.partial(backward_kernel, parts),
        in_specs=[LOCAL] * (parts + 5),
        out_specs=[LOCAL] * parts,
        out_shape=[jax.ShapeDtypeStruct((CAP, width), BF16)] * parts,
        compiler_params=PARAMS,
        cost_estimate=cost(6 * count * units * width, 6 * units * width),
        name="backward",
    )(*blocks, w_down, w_gate, w_up, pre_gate, pre_up)


def combine_kernel(parts, pieces, *refs):
    picks, blocks, out, held, sems = refs[0], refs[1 : 1 + parts], *refs[1 + parts :]
    width = out.shape[1]
    step = width // pieces
    left = jnp.where(picks[...] > 0.0, 1.0, 0.0).astype(BF16)
    if left.shape[0] < parts * CAP:
        left = rows_of([left] * parts)
    copies = []
    for piece in range(pieces):
        at = slice(piece * step, (piece + 1) * step)
        rows = rows_of([block[:, at] for block in blocks])
        held[:, at] = lax.dot_general(left, rows, TN, preferred_element_type=F32).astype(BF16)
        copy = pltpu.make_async_copy(held.at[:, at], out.at[:, at], sems.at[piece])
        copy.start()
        copies.append(copy)
    for copy in copies:
        copy.wait()


def combine(picks, blocks):
    count, tok = picks.shape
    width = blocks[0].shape[1]
    pieces = 4
    return pl.pallas_call(
        functools.partial(combine_kernel, len(blocks), pieces),
        in_specs=[LOCAL] * (1 + len(blocks)),
        out_specs=FAR,
        out_shape=jax.ShapeDtypeStruct((tok, width), BF16),
        scratch_shapes=[pltpu.VMEM((tok, width), BF16), pltpu.SemaphoreType.DMA((pieces,))],
        compiler_params=PARAMS,
        cost_estimate=cost(2 * count * tok * width, 2 * tok * width),
        name="combine",
    )(picks, *blocks)


def place_kernel(groups, *refs):
    me = lax.axis_index("grp")
    half = groups // 2
    blocks, (out, sems) = refs[: groups + half], refs[groups + half :]
    units, columns = blocks[0].shape
    copies = []
    for number, block in enumerate(blocks):
        rows = block.shape[0]
        peer = number if number < groups else number - half
        start = pl.multiple_of((me ^ peer) * columns, 128)
        at = pl.ds(0 if number < groups else units - rows, rows)
        target = out.at[at, pl.ds(start, columns)]
        copies.append(pltpu.make_async_copy(block, target, sems.at[number]))
        copies[-1].start()
    for copy in copies:
        copy.wait()


def place_blocks(groups, blocks):
    units, columns = blocks[0].shape
    return pl.pallas_call(
        functools.partial(place_kernel, groups),
        in_specs=[LOCAL] * len(blocks),
        out_specs=FAR,
        out_shape=jax.ShapeDtypeStruct((units, groups * columns), BF16),
        scratch_shapes=[pltpu.SemaphoreType.DMA((len(blocks),))],
        compiler_params=PARAMS,
        cost_estimate=cost(0, 4 * groups * units * columns),
        name="place_blocks",
    )(*blocks)


def swap(value, axis, size, bits):
    return lax.ppermute(value, axis, [(i, i ^ bits) for i in range(size)])


def body(
    tokens,
    expert_ids,
    gate_probs,
    placement,
    gate_weight,
    up_weight,
    down_weight,
    out_grad,
    moment_first,
    moment_second,
):
    num_ep = lax.axis_size("ep")
    groups = lax.axis_size("grp")
    slots = num_ep // QUARTERS
    ep_index = lax.axis_index("ep")

    def slot_of(bits):
        return (ep_index ^ bits) // QUARTERS

    def of_slot(value, bits, axis):
        if slots == 1:
            return lax.squeeze(value, (axis,))
        return lax.dynamic_index_in_dim(value, slot_of(bits), axis, keepdims=False)

    def share(value, axis):
        got = [None] * num_ep
        for far in range(0, num_ep, 2):
            piece = of_slot(value, far, axis)
            got[far] = swap(piece, "ep", num_ep, far) if far else piece
        for far in range(0, num_ep, 2):
            got[far + 1] = swap(got[far], "ep", num_ep, 1)
        return got

    def exchange(values):
        got = [values[0]]
        for bits in range(1, len(values)):
            got.append(swap(values[bits], "grp", groups, bits))
        return got

    def per_slot(value):
        return value.reshape((slots, CAP) + value.shape[1:])

    w_gate = gate_weight[0].T
    w_up = up_weight[0].T
    w_down = down_weight[0]

    rows, picks = select(placement, expert_ids.T, gate_probs.T, tokens, slots)
    in_rows = share(per_slot(rows), 0)
    scaled, *blocks = scale(picks, out_grad, groups)
    if slots > 1:
        picks = [of_slot(per_slot(picks), bits, 0) for bits in range(num_ep)]
        picks = jnp.concatenate(picks, axis=0)
    pairs = [blocks[0]]
    for number in range(1, groups // 2):
        pairs.append(swap(blocks[number], "grp", groups, 2 * number))
    kept, passed = stack(pairs)
    passed = swap(passed, "grp", groups, 1)
    columns = join(kept, passed)
    columns = columns.reshape(groups, slots, CAP, columns.shape[-1])
    near = []
    for far in range(0, num_ep, 2):
        piece = of_slot(columns, far, 1)
        near.append(swap(piece, "ep", num_ep, far) if far else piece)
    near = functools.reduce(join, near)
    columns = (near, swap(near, "ep", num_ep, 1))
    my_cand = placement
    if slots > 1:
        my_cand = lax.dynamic_index_in_dim(placement, slot_of(0), 1, keepdims=True)
    pre_gate, pre_up, hidden = forward(my_cand, in_rows, w_gate, w_up)
    hiddens = [hidden]
    for bits in range(2, groups, 2):
        hiddens.append(swap(hidden, "grp", groups, bits))
    hiddens = pile(hiddens)
    hiddens = (hiddens, swap(hiddens, "grp", groups, 1))
    summed, *dirs, both = adam(hiddens, columns, moment_first, moment_second)
    got_dirs = exchange(dirs)
    both = swap(both, "grp", groups, groups // 2)
    dirs = choose(hiddens, both)
    got_dirs = got_dirs + exchange(dirs)
    new_first, new_second = update(summed, moment_first, moment_second)

    in_scaled = share(per_slot(scaled), 0)
    partials = backward(in_scaled, w_down, w_gate, w_up, pre_gate, pre_up)
    returned = [partials[0]]
    for bits in range(1, num_ep):
        returned.append(swap(partials[bits], "ep", num_ep, bits))
    token_grad = combine(picks, returned)
    step_dir = place_blocks(groups, got_dirs)[None]
    return (token_grad, step_dir, new_first, new_second)


def solution(mesh):
    return jax.shard_map(
        body,
        mesh=mesh,
        in_specs=(
            P(("grp", "ep"), None),
            P(("grp", "ep"), None),
            P(("grp", "ep"), None),
            P("grp", None),
            P("grp", None, "ep"),
            P("grp", None, "ep"),
            P("grp", "ep", None),
            P(("grp", "ep"), None),
            P(None, "ep", "grp"),
            P(None, "ep", "grp"),
        ),
        out_specs=(
            P(("grp", "ep"), None),
            P("grp", "ep", None),
            P(None, "ep", "grp"),
            P(None, "ep", "grp"),
        ),
        check_vma=False,
    )
```

```python
import functools
import math

import jax
import jax.numpy as jnp
from jax import lax
from jax.experimental import pallas as pl
from jax.experimental.pallas import tpu as pltpu
from jax.sharding import PartitionSpec as P


QUARTERS = 4
CANDS = 2
CAP = 24
TAG = 8


beta_one = 0.9
beta_two = 0.999
adam_eps = 1e-08
first_fix = 1.0 - math.exp(1000.0 * math.log(0.9))
second_fix = 1.0 - math.exp(1000.0 * math.log(0.999))

F32 = jnp.float32
BF16 = jnp.bfloat16
NT = (((1,), (1,)), ((), ()))
TN = (((0,), (0,)), ((), ()))


SCALARS = pl.BlockSpec(memory_space=pltpu.SMEM)
LOCAL = pl.BlockSpec(memory_space=pltpu.VMEM)
FAR = pl.BlockSpec(memory_space=pltpu.HBM)
PARAMS = pltpu.CompilerParams(vmem_limit_bytes=12 * 2**20)
GRANT1 = pltpu.CompilerParams(vmem_limit_bytes=65_400_000)
GRANT2 = pltpu.CompilerParams(vmem_limit_bytes=56_000_000)


def cost(flops, moved):
    return pl.CostEstimate(flops=int(flops), bytes_accessed=int(moved) * 16, transcendentals=0)


def rows_of(parts):
    return jnp.concatenate([part.astype(F32) for part in parts], axis=0).astype(BF16)


def select_kernel(slots, pieces, place, ids, probs, tokens, rows, picks, *refs):
    ids_in, probs_in, tokens_in, sems = refs
    tok, width = tokens.shape
    step = width // pieces
    at = [slice(piece * step, (piece + 1) * step) for piece in range(pieces)]
    pairs = [(ids, ids_in), (probs, probs_in)]
    pairs += [(tokens.at[:, at[i]], tokens_in.at[:, at[i]]) for i in range(pieces)]
    copies = []
    for number, (source, target) in enumerate(pairs):
        copies.append(pltpu.make_async_copy(source, target, sems.at[number]))
        copies[-1].start()
    below = lax.broadcasted_iota(jnp.int32, (tok, tok), 0)
    right = lax.broadcasted_iota(jnp.int32, (tok, tok), 1)
    upper = jnp.where(below <= right, 1.0, 0.0).astype(BF16)
    want = lax.broadcasted_iota(jnp.int32, (CAP, tok), 0).astype(F32) + 1.0
    for copy in copies[:2]:
        copy.wait()
    chosen_list = []
    for slot in range(slots):
        expert = place[0, slot] * slots + slot
        match = ids_in[...] == expert
        hit = jnp.max(jnp.where(match, 1.0, 0.0), axis=0, keepdims=True)
        coef = jnp.sum(jnp.where(match, probs_in[...], 0.0), axis=0, keepdims=True)
        rank = jnp.dot(hit.astype(BF16), upper, preferred_element_type=F32)
        chosen = jnp.where((rank == want) & (hit > 0.0), 1.0, 0.0)
        chosen_list.append(chosen)
        picks[slot * CAP : (slot + 1) * CAP, :] = chosen * coef
    left = jnp.concatenate(chosen_list, axis=0) if slots > 1 else chosen_list[0]
    left = left.astype(BF16)
    for i in range(pieces):
        copies[2 + i].wait()
        picked = jnp.dot(left, tokens_in[:, at[i]], preferred_element_type=F32)
        rows[:, at[i]] = picked.astype(BF16)


def select(placement, ids, probs, tokens, slots):
    tok, width = tokens.shape
    pieces = 4
    count = slots * CAP
    return pl.pallas_call(
        functools.partial(select_kernel, slots, pieces),
        in_specs=[SCALARS] + [FAR] * 3,
        out_specs=[LOCAL] * 2,
        out_shape=[
            jax.ShapeDtypeStruct((count, width), BF16),
            jax.ShapeDtypeStruct((count, tok), F32),
        ],
        scratch_shapes=[
            pltpu.VMEM(ids.shape, ids.dtype),
            pltpu.VMEM(probs.shape, probs.dtype),
            pltpu.VMEM((tok, width), BF16),
            pltpu.SemaphoreType.DMA((2 + pieces,)),
        ],
        compiler_params=GRANT1,
        cost_estimate=cost(2 * count * tok * width, tok * width * 2),
        name="select_rows",
    )(placement, ids, probs, tokens)


def scale_kernel(pieces, picks, grads, scaled, *refs):
    me = lax.axis_index("grp")
    blocks, (grads_in, sems) = refs[:-2], refs[-2:]
    groups = 2 * len(blocks)
    width = grads.shape[1]
    block, step = width // groups, width // pieces
    at = [slice(piece * step, (piece + 1) * step) for piece in range(pieces)]
    copies = []
    for i in range(pieces):
        copies.append(
            pltpu.make_async_copy(grads.at[:, at[i]], grads_in.at[:, at[i]], sems.at[i])
        )
        copies[-1].start()
    coefs = jnp.sum(picks[...], axis=1, keepdims=True)
    left = jnp.where(picks[...] > 0.0, 1.0, 0.0).astype(BF16)
    for i in range(pieces):
        copies[i].wait()
        picked = jnp.dot(left, grads_in[:, at[i]], preferred_element_type=F32)
        scaled[:, at[i]] = (coefs * picked).astype(BF16)
    for group in range(groups):
        start = pl.multiple_of((me ^ group) * block, 128)
        blocks[group // 2][group % 2] = scaled[:, pl.ds(start, block)]


def scale(picks, grads, groups):
    tok, width = grads.shape
    pieces = 4
    count = picks.shape[0]
    pairs = groups // 2
    return pl.pallas_call(
        functools.partial(scale_kernel, pieces),
        in_specs=[LOCAL, FAR],
        out_specs=[LOCAL] * (1 + pairs),
        out_shape=[jax.ShapeDtypeStruct((count, width), BF16)]
        + [jax.ShapeDtypeStruct((2, count, width // groups), BF16)] * pairs,
        scratch_shapes=[pltpu.VMEM((tok, width), BF16), pltpu.SemaphoreType.DMA((pieces,))],
        compiler_params=GRANT2,
        cost_estimate=cost(2 * count * tok * width, tok * width * 8),
        name="scale_rows",
    )(picks, grads)


def stack_kernel(count, *refs):
    for number in range(count):
        for pick, out in enumerate(refs[count:]):
            out[number] = refs[number][pick]


def stack(pairs):
    shape = (len(pairs),) + pairs[0].shape[1:]
    return pl.pallas_call(
        functools.partial(stack_kernel, len(pairs)),
        in_specs=[LOCAL] * len(pairs),
        out_specs=[LOCAL] * 2,
        out_shape=[jax.ShapeDtypeStruct(shape, BF16)] * 2,
        compiler_params=PARAMS,
        cost_estimate=cost(0, 2 * len(pairs) * pairs[0].size),
        name="stack",
    )(*pairs)


def pile_kernel(count, *refs):
    for number in range(count):
        refs[count][number] = refs[number][...]


def pile(blocks):
    return pl.pallas_call(
        functools.partial(pile_kernel, len(blocks)),
        in_specs=[LOCAL] * len(blocks),
        out_specs=LOCAL,
        out_shape=jax.ShapeDtypeStruct((len(blocks),) + blocks[0].shape, BF16),
        compiler_params=PARAMS,
        cost_estimate=cost(0, 4 * len(blocks) * blocks[0].size),
        name="pile",
    )(*blocks)


def join_kernel(one, two, out):
    count = one.shape[0]
    out[0:count] = one[...]
    out[count:] = two[...]


def join(one, two):
    shape = (one.shape[0] + two.shape[0],) + one.shape[1:]
    return pl.pallas_call(
        join_kernel,
        in_specs=[LOCAL] * 2,
        out_specs=LOCAL,
        out_shape=jax.ShapeDtypeStruct(shape, BF16),
        compiler_params=PARAMS,
        cost_estimate=cost(0, 8 * one.size),
        name="join",
    )(one, two)


def forward_kernel(parts, place, *refs):
    blocks, (w_gate, w_up, pre_gate, pre_up, hidden) = refs[:parts], refs[parts:]
    inputs = rows_of([block[...] for block in blocks])
    gate = lax.dot_general(inputs, w_gate[...], NT, preferred_element_type=F32)
    up = lax.dot_general(inputs, w_up[...], NT, preferred_element_type=F32)
    pre_gate[...] = gate
    pre_up[...] = up
    count = gate.shape[0]
    hidden[0:count, :] = (gate * jax.nn.sigmoid(gate) * up).astype(BF16)
    tag = place[0, 0].astype(F32)
    hidden[count : count + TAG, :] = jnp.full((TAG, gate.shape[1]), tag, F32).astype(BF16)


def forward(my_cand, blocks, w_gate, w_up):
    units, width = w_gate.shape
    count = len(blocks) * CAP
    return pl.pallas_call(
        functools.partial(forward_kernel, len(blocks)),
        in_specs=[SCALARS] + [LOCAL] * (len(blocks) + 2),
        out_specs=[LOCAL] * 3,
        out_shape=[
            jax.ShapeDtypeStruct((count, units), F32),
            jax.ShapeDtypeStruct((count, units), F32),
            jax.ShapeDtypeStruct((count + TAG, units), BF16),
        ],
        compiler_params=PARAMS,
        cost_estimate=cost(4 * count * units * width, 4 * units * width),
        name="forward",
    )(my_cand, *blocks, w_gate, w_up)


def adam_kernel(groups, parts, *refs):
    half = groups // 2
    hiddens, refs = [refs[p % 2].at[p // 2] for p in range(groups)], refs[2:]
    near, other, first, second, summed = refs[:5]
    dirs = refs[5:]
    count = parts * CAP
    rights = []
    lefts = [[] for _ in range(CANDS)]
    for peer in range(groups):
        held = hiddens[peer]
        part_rows = held[0:count, :].astype(F32)
        tag = held[count : count + TAG, :].astype(F32)[0:1, :]
        for cand in range(CANDS):
            lefts[cand].append(jnp.where(tag == float(cand), part_rows, 0.0))
        for part in range(parts):
            stack = (near, other)[part % 2]
            at = part // 2 * groups + peer // 2 + peer % 2 * half
            rights.append(stack[at].astype(F32))
    right = jnp.concatenate(rights, axis=0).astype(BF16)
    dir_list = []
    for cand in range(CANDS):
        left = jnp.concatenate(lefts[cand], axis=0).astype(BF16)
        grad = lax.dot_general(left, right, TN, preferred_element_type=F32)
        summed[cand] = grad
        one, two = moments(grad, first[cand], second[cand])
        dir_list.append(one / first_fix / (jnp.sqrt(two / second_fix) + adam_eps))
    both = dirs[groups]
    split = dir_list[0].shape[0] - both.shape[1]
    for cand in range(CANDS):
        both[cand] = dir_list[cand][split:].astype(BF16)
    for peer in range(groups):
        tag = hiddens[peer][count : count + TAG, :].astype(F32)[0:1, 0:1]
        out = dir_list[0]
        for cand in range(1, CANDS):
            out = jnp.where(tag == float(cand), dir_list[cand], out)
        dirs[peer][...] = out[: dirs[peer].shape[0]].astype(BF16)


def moments(gradient, first_moment, second):
    new_first = beta_one * first_moment + (1.0 - beta_one) * gradient
    new_second = beta_two * second + (1.0 - beta_two) * gradient * gradient
    return (new_first, new_second)


def adam(hiddens, blocks, first, second):
    groups = 2 * hiddens[0].shape[0]
    parts = 2 * blocks[0].shape[0] // groups
    units, columns = first.shape[1:]
    split = units // 2
    rows = groups * parts * CAP
    return pl.pallas_call(
        functools.partial(adam_kernel, groups, parts),
        in_specs=[LOCAL] * 6,
        out_specs=[LOCAL] * (2 + groups),
        out_shape=[jax.ShapeDtypeStruct(first.shape, F32)]
        + [jax.ShapeDtypeStruct((units, columns), BF16)] * (groups // 2)
        + [jax.ShapeDtypeStruct((split, columns), BF16)] * (groups // 2)
        + [jax.ShapeDtypeStruct((CANDS, units - split, columns), BF16)],
        compiler_params=PARAMS,
        cost_estimate=cost(2 * CANDS * rows * units * columns, 8 * first.size),
        name="adam",
    )(*hiddens, *blocks, first, second)


def choose_kernel(half, *refs):
    hiddens, both, outs = [refs[p % 2].at[p // 2] for p in range(half)], refs[2], refs[3:]
    for peer in range(half):
        count = hiddens[peer].shape[0] - TAG
        tag = hiddens[peer][count : count + TAG, :].astype(F32)[0:1, 0:1]
        out = both[0].astype(F32)
        for cand in range(1, CANDS):
            out = jnp.where(tag == float(cand), both[cand].astype(F32), out)
        outs[peer][...] = out.astype(BF16)


def choose(hiddens, both):
    half = hiddens[0].shape[0]
    return pl.pallas_call(
        functools.partial(choose_kernel, half),
        in_specs=[LOCAL] * 3,
        out_specs=[LOCAL] * half,
        out_shape=[jax.ShapeDtypeStruct(both.shape[1:], BF16)] * half,
        compiler_params=PARAMS,
        cost_estimate=cost(both.size, 2 * half * both.size),
        name="choose",
    )(*hiddens, both)


def update_kernel(summed, first, second, new_first, new_second, one_out, two_out, sems):
    copies = []
    for cand in range(CANDS):
        one_out[cand], two_out[cand] = moments(summed[cand], first[cand], second[cand])
        for number, (source, target) in enumerate([(one_out, new_first), (two_out, new_second)]):
            copy = pltpu.make_async_copy(
                source.at[cand], target.at[cand], sems.at[2 * cand + number]
            )
            copy.start()
            copies.append(copy)
    for copy in copies:
        copy.wait()


def update(summed, first, second):
    return pl.pallas_call(
        update_kernel,
        in_specs=[LOCAL] * 3,
        out_specs=[FAR] * 2,
        out_shape=[jax.ShapeDtypeStruct(first.shape, F32)] * 2,
        scratch_shapes=[pltpu.VMEM(first.shape, F32)] * 2
        + [pltpu.SemaphoreType.DMA((2 * CANDS,))],
        compiler_params=PARAMS,
        cost_estimate=cost(8 * first.size, 8 * first.size),
        name="update",
    )(summed, first, second)


def backward_kernel(parts, *refs):
    blocks, refs = refs[:parts], refs[parts:]
    w_down, w_gate, w_up, pre_gate, pre_up = refs[:5]
    outs = refs[5:]
    inputs = rows_of([block[...] for block in blocks])
    d_hidden = lax.dot_general(inputs, w_down[...], NT, preferred_element_type=F32)
    gate, up = pre_gate[...], pre_up[...]
    sig = jax.nn.sigmoid(gate)
    d_gate = (d_hidden * up * sig * (1.0 + gate * (1.0 - sig))).astype(BF16)
    d_up = (d_hidden * (gate * sig)).astype(BF16)
    width = w_gate.shape[1]
    step = width // 4
    for piece in range(4):
        at = slice(piece * step, (piece + 1) * step)
        out = jnp.dot(d_gate, w_gate[:, at], preferred_element_type=F32)
        out = out + jnp.dot(d_up, w_up[:, at], preferred_element_type=F32)
        for part in range(parts):
            outs[part][:, at] = out[part * CAP : (part + 1) * CAP, :].astype(BF16)


def backward(blocks, w_down, w_gate, w_up, pre_gate, pre_up):
    units, width = w_down.shape
    parts = len(blocks)
    count = parts * CAP
    return pl.pallas_call(
        functools.partial(backward_kernel, parts),
        in_specs=[LOCAL] * (parts + 5),
        out_specs=[LOCAL] * parts,
        out_shape=[jax.ShapeDtypeStruct((CAP, width), BF16)] * parts,
        compiler_params=PARAMS,
        cost_estimate=cost(6 * count * units * width, 6 * units * width),
        name="backward",
    )(*blocks, w_down, w_gate, w_up, pre_gate, pre_up)


def combine_kernel(parts, pieces, *refs):
    picks, blocks, out, held, sems = refs[0], refs[1 : 1 + parts], *refs[1 + parts :]
    width = out.shape[1]
    step = width // pieces
    left = jnp.where(picks[...] > 0.0, 1.0, 0.0).astype(BF16)
    if left.shape[0] < parts * CAP:
        left = rows_of([left] * parts)
    copies = []
    for piece in range(pieces):
        at = slice(piece * step, (piece + 1) * step)
        rows = rows_of([block[:, at] for block in blocks])
        held[:, at] = lax.dot_general(left, rows, TN, preferred_element_type=F32).astype(BF16)
        copy = pltpu.make_async_copy(held.at[:, at], out.at[:, at], sems.at[piece])
        copy.start()
        copies.append(copy)
    for copy in copies:
        copy.wait()


def combine(picks, blocks):
    count, tok = picks.shape
    width = blocks[0].shape[1]
    pieces = 4
    return pl.pallas_call(
        functools.partial(combine_kernel, len(blocks), pieces),
        in_specs=[LOCAL] * (1 + len(blocks)),
        out_specs=FAR,
        out_shape=jax.ShapeDtypeStruct((tok, width), BF16),
        scratch_shapes=[pltpu.VMEM((tok, width), BF16), pltpu.SemaphoreType.DMA((pieces,))],
        compiler_params=PARAMS,
        cost_estimate=cost(2 * count * tok * width, 2 * tok * width),
        name="combine",
    )(picks, *blocks)


def place_kernel(peers, fold, *refs):
    me = lax.axis_index("grp")
    count = len(peers)
    blocks, (out, sems) = refs[:count], refs[-2:]
    columns = blocks[0].shape[1]
    copies = []
    for number, block in enumerate(blocks):
        rows = block.shape[0]
        start = pl.multiple_of((me ^ peers[number]) * columns, 128)
        at = pl.ds(out.shape[0] - rows if fold else 0, rows)
        target = out.at[at, pl.ds(start, columns)]
        copies.append(pltpu.make_async_copy(block, target, sems.at[number]))
        copies[-1].start()
    for copy in copies:
        copy.wait()


def place_blocks(peers, blocks, shape, placed=None):
    fold = placed is not None
    count = len(blocks)
    return pl.pallas_call(
        functools.partial(place_kernel, peers, fold),
        in_specs=[LOCAL] * count + [FAR] * fold,
        out_specs=FAR,
        out_shape=jax.ShapeDtypeStruct(shape, BF16),
        scratch_shapes=[pltpu.SemaphoreType.DMA((count,))],
        input_output_aliases={count: 0} if fold else {},
        compiler_params=PARAMS,
        cost_estimate=cost(0, 4 * shape[0] * shape[1]),
        name="place_last" if fold else "place_first",
    )(*blocks, *([placed] if fold else []))


def swap(value, axis, size, bits):
    return lax.ppermute(value, axis, [(i, i ^ bits) for i in range(size)])


def body(
    tokens,
    expert_ids,
    gate_probs,
    placement,
    gate_weight,
    up_weight,
    down_weight,
    out_grad,
    moment_first,
    moment_second,
):
    num_ep = lax.axis_size("ep")
    groups = lax.axis_size("grp")
    slots = num_ep // QUARTERS
    ep_index = lax.axis_index("ep")

    def slot_of(bits):
        return (ep_index ^ bits) // QUARTERS

    def of_slot(value, bits, axis):
        if slots == 1:
            return lax.squeeze(value, (axis,))
        return lax.dynamic_index_in_dim(value, slot_of(bits), axis, keepdims=False)

    def share(value, axis):
        got = [None] * num_ep
        for far in range(0, num_ep, 2):
            piece = of_slot(value, far, axis)
            got[far] = swap(piece, "ep", num_ep, far) if far else piece
        for far in range(0, num_ep, 2):
            got[far + 1] = swap(got[far], "ep", num_ep, 1)
        return got

    def exchange(values):
        got = [values[0]]
        for bits in range(1, len(values)):
            got.append(swap(values[bits], "grp", groups, bits))
        return got

    def per_slot(value):
        return value.reshape((slots, CAP) + value.shape[1:])

    w_gate = gate_weight[0].T
    w_up = up_weight[0].T
    w_down = down_weight[0]

    rows, picks = select(placement, expert_ids.T, gate_probs.T, tokens, slots)
    in_rows = share(per_slot(rows), 0)
    scaled, *blocks = scale(picks, out_grad, groups)
    if slots > 1:
        picks = [of_slot(per_slot(picks), bits, 0) for bits in range(num_ep)]
        picks = jnp.concatenate(picks, axis=0)
    pairs = [blocks[0]]
    for number in range(1, groups // 2):
        pairs.append(swap(blocks[number], "grp", groups, 2 * number))
    kept, passed = stack(pairs)
    passed = swap(passed, "grp", groups, 1)
    columns = join(kept, passed)
    columns = columns.reshape(groups, slots, CAP, columns.shape[-1])
    near = []
    for far in range(0, num_ep, 2):
        piece = of_slot(columns, far, 1)
        near.append(swap(piece, "ep", num_ep, far) if far else piece)
    near = functools.reduce(join, near)
    columns = (near, swap(near, "ep", num_ep, 1))
    my_cand = placement
    if slots > 1:
        my_cand = lax.dynamic_index_in_dim(placement, slot_of(0), 1, keepdims=True)
    pre_gate, pre_up, hidden = forward(my_cand, in_rows, w_gate, w_up)
    hiddens = [hidden]
    for bits in range(2, groups, 2):
        hiddens.append(swap(hidden, "grp", groups, bits))
    hiddens = pile(hiddens)
    hiddens = (hiddens, swap(hiddens, "grp", groups, 1))
    summed, *dirs, both = adam(hiddens, columns, moment_first, moment_second)
    got_dirs = exchange(dirs)
    both = swap(both, "grp", groups, groups // 2)
    dirs = choose(hiddens, both)
    passed_dirs = exchange(dirs)
    new_first, new_second = update(summed, moment_first, moment_second)

    in_scaled = share(per_slot(scaled), 0)
    partials = backward(in_scaled, w_down, w_gate, w_up, pre_gate, pre_up)
    returned = [partials[0]]
    for bits in range(1, num_ep):
        returned.append(swap(partials[bits], "ep", num_ep, bits))
    token_grad = combine(picks, returned)
    units, columns = got_dirs[0].shape
    shape = (units, groups * columns)
    peers = list(range(groups))
    placed = place_blocks(peers, got_dirs, shape)
    step_dir = place_blocks(peers[groups // 2 :], passed_dirs, shape, placed)[None]
    return (token_grad, step_dir, new_first, new_second)


def solution(mesh):
    return jax.shard_map(
        body,
        mesh=mesh,
        in_specs=(
            P(("grp", "ep"), None),
            P(("grp", "ep"), None),
            P(("grp", "ep"), None),
            P("grp", None),
            P("grp", None, "ep"),
            P("grp", None, "ep"),
            P("grp", "ep", None),
            P(("grp", "ep"), None),
            P(None, "ep", "grp"),
            P(None, "ep", "grp"),
        ),
        out_specs=(
            P(("grp", "ep"), None),
            P("grp", "ep", None),
            P(None, "ep", "grp"),
            P(None, "ep", "grp"),
        ),
        check_vma=False,
    )
```
